128 devices in a mesh: row: 8 (over y, z_lo), col: 16 (over x, z_hi, core).
Axes of the slice: x: 4, y: 4, z: 4 (z_hi: 2, z_lo: 2; z = z_hi * 2 + z_lo), core: 2. Of those that a mesh axis runs over, the one named last changes fastest.
Arguments:
- tokens: bfloat16 [1024, 53248], P(('row', 'col')), may hold values from -6 to 6
- eigvecs: float32 [53248, 2048], P('row', 'col'), may hold values from -0.02734375 to 0.02734375
- eigvals: float32 [2048], P('col'), may hold values from 0.25 to 4
- v_first: float32 [53248, 256], P(('row', 'col')), may hold values from -0.109375 to 0.109375
- v_second: float32 [53248, 256], P(('row', 'col')), may hold values from -0.109375 to 0.109375
- t_first: float32 [256, 256], replicated, may hold values from -0.375 to 0.375
- t_second: float32 [256, 256], replicated, may hold values from -0.375 to 0.375
Outputs:
- whitened: float32 [1024, 2048], P('row', 'col')
The draws below stay inside these ranges and needn't reach their ends.
All inputs are finite; a program needn't handle non-finite values.
Results may differ from the reference program's by a relative error of at most 0.0029.
Values may be sent and summed in bfloat16 or wider, within the bound.
A program may use at most 128 MiB of HBM per device.

```python
import math
import jax
import jax.numpy as jnp
from jax import lax

D = 53248
K = 2048
NB = 256
TOK = 1024


def shard_levels(own_key, dims, shards, smallest, top_value):
    loudness, own = 1.0, jax.random.fold_in(own_key, 6)
    for axis_at, parts in shards:
        heights = jnp.exp(jax.random.uniform(jax.random.fold_in(own, axis_at), (parts,), jnp.float32, smallest / len(shards), top_value / len(shards)))
        loudness = loudness * jnp.repeat(heights, dims[axis_at] // parts).reshape([-1 if axis == axis_at else 1 for axis in range(len(dims))])
    return loudness


def noise(own_key, shape, deviation, bound, split=(), held_as=jnp.bfloat16):
    values = jax.random.normal(own_key, shape, jnp.float32) * deviation
    if len(split) > 0:
        values = shard_levels(own_key, shape, split, -0.22, 0.18) * values
    return jnp.clip(values, min=-bound, max=bound).astype(held_as)


def setup_inputs(seed: int = 0) -> dict:
    splits = jax.random.split(jax.random.key(seed), 8)
    tokens = noise(splits[0], (TOK, D), 1.0, 6.0, ((0, 128),))
    eigvecs = noise(splits[1], (D, K), D ** -0.5, 0.02734375, ((0, 8), (1, 16)), jnp.float32)
    eigvals = jnp.clip(jnp.exp(math.log(4.0) - 2.7725887 * jax.random.uniform(splits[2], (K,), jnp.float32) ** shard_levels(splits[2], (K,), ((0, 16),), -0.2, 0.2)), 0.25, 4.0)
    v_first = noise(splits[3], (D, NB), (D // 16) ** -0.5, 0.109375, ((0, 128),), jnp.float32)
    v_second = noise(splits[4], (D, NB), (D // 16) ** -0.5, 0.109375, ((0, 128),), jnp.float32)
    t_first = noise(splits[5], (NB, NB), NB ** -0.5, 0.375, (), jnp.float32)
    t_second = noise(splits[6], (NB, NB), NB ** -0.5, 0.375, (), jnp.float32)
    return dict(tokens=tokens, eigvecs=eigvecs, eigvals=eigvals, v_first=v_first, v_second=v_second, t_first=t_first, t_second=t_second)


def reflect(block, panel, factor):
    inner = jnp.dot(panel.T, block, precision=lax.Precision.HIGHEST, preferred_element_type=jnp.float32)
    middle = jnp.dot(factor, inner, precision=lax.Precision.HIGHEST, preferred_element_type=jnp.float32)
    return block - jnp.dot(panel, middle, precision=lax.Precision.HIGHEST, preferred_element_type=jnp.float32)

def reference(tokens, eigvecs, eigvals, v_first, v_second, t_first, t_second):
    rotated = reflect(eigvecs, v_second, t_second)
    rotated = reflect(rotated, v_first, t_first)
    whitening = (rotated * lax.rsqrt(eigvals)[None, :]).astype(jnp.bfloat16)
    return jnp.dot(tokens, whitening, preferred_element_type=jnp.float32)
```

```python
import functools

import jax
import jax.numpy as jnp
from jax import lax
from jax.experimental import pallas as pl
from jax.experimental.pallas import tpu as pltpu
from jax.sharding import PartitionSpec as P

MESH = pl.DeviceIdType.MESH
BF16 = jnp.bfloat16
F32 = jnp.float32
HIGH = lax.Precision.HIGHEST

ROWS = 1664
OWN = 416
SLAB = 6656
YSEG = 2 * SLAB
COPIES = 96


def mm(a, b):
    return jnp.dot(a, b, preferred_element_type=F32)


def exact(a, b):
    return jnp.dot(a, b, precision=HIGH, preferred_element_type=F32)


def kernel(
    x_ref, e_ref, v1_ref, v2_ref, t1_ref, t2_ref, ev_ref, out_ref,
    xy, xs, xb, x2, es, eb, vb, vt, vq, vc,
    p, ry, s, rz, s2, rx, xv,
    pv, rv, sv, rvz, sv2, rvx, u, g,
    send, recv, local,
):
    r, c = lax.axis_index("row"), lax.axis_index("col")
    y, zlo = r // 2, r % 2
    x, q = c // 4, c % 4
    zhi, k = q // 2, q % 2

    def at_y(d):
        return (((y + d) % 4) * 2 + zlo, c)

    def at_x(d):
        return (r, ((x + d) % 4) * 4 + q)

    z_far = (r, x * 4 + (1 - zhi) * 2 + k)
    z_near = (y * 2 + 1 - zlo, c)
    z_other = (y * 2 + 1 - zlo, x * 4 + (1 - zhi) * 2 + k)
    sibling = (r, x * 4 + zhi * 2 + 1 - k)

    peers = [at_y(1), at_y(2), at_y(3), at_x(1), at_x(2), at_x(3)]
    peers += [z_far, z_near, z_other, sibling]
    barrier = pltpu.get_barrier_semaphore()
    for peer in peers:
        pl.semaphore_signal(barrier, inc=1, device_id=peer, device_id_type=MESH)

    started = []

    def put(src, dst, device):
        slot = len(started)
        copy = pltpu.make_async_remote_copy(
            src_ref=src, dst_ref=dst, send_sem=send.at[slot], recv_sem=recv.at[slot],
            device_id=device, device_id_type=MESH,
        )
        copy.start()
        started.append(copy)
        return copy

    here = []

    def move(src, dst):
        copy = pltpu.make_async_copy(src, dst, local.at[len(here)])
        copy.start()
        here.append(copy)
        return copy

    for chunk in range(4):
        panel = v2_ref if chunk < 2 else v1_ref
        value = panel[:, (chunk % 2) * 128 : (chunk % 2 + 1) * 128]
        high = value.astype(BF16)
        vb[0, chunk, q] = high
        vb[1, chunk, q] = (value - high.astype(F32)).astype(BF16)

    def cast(i, carry):
        at = pl.ds(pl.multiple_of(i * 208, 208), 208)
        es[at] = e_ref[at].astype(BF16)
        return carry

    lax.fori_loop(0, 32, cast, 0)

    pl.semaphore_wait(barrier, len(peers))

    y_in = {}
    for d in (2, 1, 3):
        to = (y + d) % 4
        src = x_ref.at[:, pl.ds(pl.multiple_of(to * YSEG, 128), YSEG)]
        y_in[d] = put(src, xy.at[d - 1], at_y(d))
    v_far = put(vb.at[:, :, q], vb.at[:, :, q], z_far)
    v_sib = put(vb.at[:, :, q], vb.at[:, :, q], sibling)
    own_cols = pl.ds(pl.multiple_of(x * 128, 128), 128)
    e_in = []
    for e in (2, 1, 3):
        to = (x + e) % 4
        src = es.at[pl.ds(pl.multiple_of(to * ROWS, ROWS), ROWS)]
        e_in.append(put(src, eb.at[:, own_cols], at_x(e)))
    e_own = move(es.at[pl.ds(pl.multiple_of(x * ROWS, ROWS), ROWS)], eb.at[:, own_cols])

    def x_stage(d):
        def piece(zl, to):
            at = zl * SLAB + to * ROWS
            if d == 0:
                return x_ref.at[:, pl.ds(pl.multiple_of(y * YSEG + at, 128), ROWS)]
            return xy.at[d - 1, :, pl.ds(pl.multiple_of(at, 128), ROWS)]

        mine, other = xb.at[d, zlo, x, zhi, k], xs.at[d, x]
        waits = []
        for e in (2, 1, 3):
            to = (x + e) % 4
            waits.append(put(piece(zlo, to), mine, at_x(e)))
            waits.append(put(piece(1 - zlo, to), other, at_x(e)))
        return waits, [move(piece(zlo, x), mine), move(piece(1 - zlo, x), other)]

    def z_stage(d):
        block = xb.at[d, zlo, :, zhi, k]
        return [
            put(block, block, z_far),
            put(xs.at[d], block, z_near),
            put(xs.at[d], block, z_other),
        ]

    x_in, z_in, c_in = {}, {}, {}
    x_in[0] = x_stage(0)
    for d in (2, 1, 3):
        y_in[d].wait_recv()
        x_in[d] = x_stage(d)
    order = (2, 1, 3, 0)
    for d in order:
        for copy in x_in[d][0]:
            copy.wait_recv()
        for copy in x_in[d][1]:
            copy.wait()
        z_in[d] = z_stage(d)

    v_far.wait_recv()
    far = (1 - zhi) * 2 + k
    v_pass = put(vb.at[:, :, far], vb.at[:, :, far], sibling)
    v_sib.wait_recv()
    e_own.wait()
    for copy in e_in:
        copy.wait_recv()
    v_pass.wait_recv()

    for term in range(2):
        vq[:, term * 128 : (term + 1) * 128] = vb[term, q].reshape(ROWS, 128)
        vc[:, term * 128 : (term + 1) * 128] = vb[term, k].reshape(ROWS, 128)
        for chunk in range(4):
            vt[term, chunk * 128 : (chunk + 1) * 128, :] = vb[term, chunk].reshape(ROWS, 128).T
    for half in range(2):
        cols = eb[:, half * 256 : (half + 1) * 256]
        part = mm(vt[0], cols) + mm(vt[1], cols)
        pv[2 * half] = part[:, :128]
        pv[2 * half + 1] = part[:, 128:]
    both = mm(vt[0], vc[...])
    pv[4] = both[:, :128] + both[:, 128:] + mm(vt[1], vc[:, :128])

    v_in = {}
    for d in (2, 1, 3):
        to = (y - d) % 4
        rows = pl.ds(pl.multiple_of(to * 128, 128), 128)
        v_in[d] = put(pv.at[:, rows, :], rv.at[d - 1], at_y(-d))

    for d in order:
        for copy in z_in[d]:
            copy.wait_recv()
        block = xb.at[d, :, :, :, k]
        c_in[d] = put(block, block, sibling)

    def project(d):
        c_in[d].wait_recv()

        def pack(i, carry):
            rows = xb[d, i // 4, i % 4].astype(F32).reshape(32, ROWS)
            x2[pl.ds(pl.multiple_of(i * 32, 32), 32)] = rows.astype(BF16)
            return carry

        lax.fori_loop(0, 8, pack, 0)
        part = mm(x2[...], eb[...])
        for j in range(4):
            p[d, j] = part[:, j * 128 : (j + 1) * 128]
        both = mm(x2[...], vq[...])
        p[d, 4] = both[:, :128] + both[:, 128:]
        if d > 0:
            return put(p.at[d], ry.at[d - 1], at_y(-d))

    p_in = {}
    p_in[2] = project(2)
    p_in[1] = project(1)
    p_in[3] = project(3)

    for d in (1, 3, 2):
        v_in[d].wait_recv()
    own_rows = pl.ds(pl.multiple_of(y * 128, 128), 128)
    sv[...] = pv[:, own_rows, :] + rv[0] + rv[1] + rv[2]
    vz_in = put(sv.at[:, pl.ds(pl.multiple_of((1 - zlo) * 64, 64), 64), :], rvz, z_near)

    project(0)

    vz_in.wait_recv()
    sv2[...] = sv[:, pl.ds(pl.multiple_of(zlo * 64, 64), 64), :] + rvz[...]
    vx_in = []
    for e in (2, 1, 3):
        vx_in.append(put(sv2.at[(x + e) % 4], rvx.at[e - 1, 0], at_x(e)))
        vx_in.append(put(sv2.at[4], rvx.at[e - 1, 1], at_x(e)))
    for copy in vx_in:
        copy.wait_recv()
    mine = pl.ds(pl.multiple_of(r * 64, 64), 64)
    u[0, mine] = sv2[x] + rvx[0, 0] + rvx[1, 0] + rvx[2, 0]
    u[1, mine] = sv2[4] + rvx[0, 1] + rvx[1, 1] + rvx[2, 1]
    uz_in = put(u.at[:, mine], u.at[:, mine], z_near)
    uz_in.wait_recv()
    pair = pl.ds(pl.multiple_of(y * 128, 128), 128)
    uy_in = [put(u.at[:, pair], u.at[:, pair], at_y(d)) for d in (2, 1, 3)]

    for d in (2, 1, 3):
        p_in[d].wait_recv()
    for j in range(5):
        s[j] = p[0, j] + ry[0, j] + ry[1, j] + ry[2, j]
    z_sum = put(s.at[:, pl.ds(pl.multiple_of((1 - zlo) * 128, 128), 128), :], rz, z_near)

    for copy in uy_in:
        copy.wait_recv()
    g[k] = u[1, 256:512]
    g_in = put(g.at[k], g.at[k], sibling)

    z_sum.wait_recv()
    s2[...] = s[:, pl.ds(pl.multiple_of(zlo * 128, 128), 128), :] + rz[...]
    x_sum = []
    for e in (2, 1, 3):
        x_sum.append(put(s2.at[4], rx.at[e - 1, 1], at_x(e)))
        x_sum.append(put(s2.at[(x + e) % 4], rx.at[e - 1, 0], at_x(e)))

    g_in.wait_recv()
    middle_second = exact(t2_ref[...], u[0, 0:256])
    inner_first = (
        u[0, 256:512] - exact(g[0], middle_second[:128]) - exact(g[1], middle_second[128:])
    )
    middle_first = exact(t1_ref[...], inner_first)

    for copy in x_sum:
        copy.wait_recv()
    xv[q] = s2[4] + rx[0, 1] + rx[1, 1] + rx[2, 1]
    far_in = put(xv.at[q], xv.at[q], z_far)
    sib_in = put(xv.at[q], xv.at[q], sibling)
    total = s2[x] + rx[0, 0] + rx[1, 0] + rx[2, 0]
    far_in.wait_recv()
    pass_in = put(xv.at[far], xv.at[far], sibling)
    sib_in.wait_recv()
    pass_in.wait_recv()
    for j in range(4):
        middle = middle_second if j < 2 else middle_first
        total = total - exact(xv[j], middle[(j % 2) * 128 : (j % 2 + 1) * 128])
    out_ref[...] = total * lax.rsqrt(ev_ref[...])

    for copy in started:
        copy.wait_send()


def per_device(tokens, eigvecs, eigvals, v_first, v_second, t_first, t_second):
    vmem = pl.BlockSpec(memory_space=pltpu.VMEM)
    return pl.pallas_call(
        kernel,
        out_shape=jax.ShapeDtypeStruct((128, 128), F32),
        in_specs=[vmem] * 7,
        out_specs=vmem,
        scratch_shapes=[
            pltpu.VMEM((3, 8, YSEG), BF16),
            pltpu.VMEM((4, 4, 8, ROWS), BF16),
            pltpu.VMEM((4, 2, 4, 2, 2, 8, ROWS), BF16),
            pltpu.VMEM((256, ROWS), BF16),
            pltpu.VMEM((SLAB, 128), BF16),
            pltpu.VMEM((ROWS, 512), BF16),
            pltpu.VMEM((2, 4, 4, OWN, 128), BF16),
            pltpu.VMEM((2, 512, ROWS), BF16),
            pltpu.VMEM((ROWS, 256), BF16),
            pltpu.VMEM((ROWS, 256), BF16),
            pltpu.VMEM((4, 5, 256, 128), F32),
            pltpu.VMEM((3, 5, 256, 128), F32),
            pltpu.VMEM((5, 256, 128), F32),
            pltpu.VMEM((5, 128, 128), F32),
            pltpu.VMEM((5, 128, 128), F32),
            pltpu.VMEM((3, 2, 128, 128), F32),
            pltpu.VMEM((4, 128, 128), F32),
            pltpu.VMEM((5, 512, 128), F32),
            pltpu.VMEM((3, 5, 128, 128), F32),
            pltpu.VMEM((5, 128, 128), F32),
            pltpu.VMEM((5, 64, 128), F32),
            pltpu.VMEM((5, 64, 128), F32),
            pltpu.VMEM((3, 2, 64, 128), F32),
            pltpu.VMEM((2, 512, 128), F32),
            pltpu.VMEM((2, 256, 128), F32),
            pltpu.SemaphoreType.DMA((COPIES,)),
            pltpu.SemaphoreType.DMA((COPIES,)),
            pltpu.SemaphoreType.DMA((16,)),
        ],
        compiler_params=pltpu.CompilerParams(
            collective_id=0, has_side_effects=True, vmem_limit_bytes=56 * 1024 * 1024
        ),
    )(tokens, eigvecs, v_first, v_second, t_first, t_second, eigvals.reshape(1, 128))


def solution(mesh):
    in_specs = (
        P(("row", "col"), None),
        P("row", "col"),
        P("col"),
        P(("row", "col"), None),
        P(("row", "col"), None),
        P(),
        P(),
    )
    out_specs = P("row", "col")
    return jax.shard_map(
        per_device, mesh=mesh, in_specs=in_specs, out_specs=out_specs, check_vma=False
    )
```

```python
import functools

import jax
import jax.numpy as jnp
from jax import lax
from jax.experimental import pallas as pl
from jax.experimental.pallas import tpu as pltpu
from jax.sharding import PartitionSpec as P

MESH = pl.DeviceIdType.MESH
BF16 = jnp.bfloat16
F32 = jnp.float32
HIGH = lax.Precision.HIGHEST

ROWS = 1664
OWN = 416
SLAB = 6656
YSEG = 2 * SLAB
HALF = ROWS // 2
COPIES = 120


def mm(a, b):
    return jnp.dot(a, b, preferred_element_type=F32)


def exact(a, b):
    return jnp.dot(a, b, precision=HIGH, preferred_element_type=F32)


def kernel(
    x_ref, e_ref, v1_ref, v2_ref, t1_ref, t2_ref, ev_ref, out_ref,
    xy, xs, xb, x2, es, eb, vb, vt, vq, vc,
    pa, ra, sa, rxa, pb, rb, sb, ryb, ab, rab,
    px, rx, sx, rzx, s2x, rx2, xv,
    va, rva, sva, rvxa, vbp, rvb, svb, rvyb, vv, rvv, svv, rvx,
    uz, ruz, u, g,
    send, recv, local,
):
    r, c = lax.axis_index("row"), lax.axis_index("col")
    y, zlo = r // 2, r % 2
    x, q = c // 4, c % 4
    zhi, k = q // 2, q % 2

    def at_y(d):
        return (((y + d) % 4) * 2 + zlo, c)

    def at_x(d):
        return (r, ((x + d) % 4) * 4 + q)

    z_far = (r, x * 4 + (1 - zhi) * 2 + k)
    z_near = (y * 2 + 1 - zlo, c)
    z_other = (y * 2 + 1 - zlo, x * 4 + (1 - zhi) * 2 + k)
    sibling = (r, x * 4 + zhi * 2 + 1 - k)

    peers = [at_y(1), at_y(2), at_y(3), at_x(1), at_x(2), at_x(3)]
    peers += [z_far, z_near, z_other, sibling]
    barrier = pltpu.get_barrier_semaphore()
    for peer in peers:
        pl.semaphore_signal(barrier, inc=1, device_id=peer, device_id_type=MESH)

    started = []

    def put(src, dst, device):
        slot = len(started)
        copy = pltpu.make_async_remote_copy(
            src_ref=src, dst_ref=dst, send_sem=send.at[slot], recv_sem=recv.at[slot],
            device_id=device, device_id_type=MESH,
        )
        copy.start()
        started.append(copy)
        return copy

    here = []

    def move(src, dst):
        copy = pltpu.make_async_copy(src, dst, local.at[len(here)])
        copy.start()
        here.append(copy)
        return copy

    def arrived(copies):
        for copy in copies:
            copy.wait_recv()

    def rows(start, size):
        return pl.ds(pl.multiple_of(start, size), size)

    for chunk in range(4):
        panel = v2_ref if chunk < 2 else v1_ref
        value = panel[:, (chunk % 2) * 128 : (chunk % 2 + 1) * 128]
        high = value.astype(BF16)
        vb[0, chunk, q] = high
        vb[1, chunk, q] = (value - high.astype(F32)).astype(BF16)

    def cast(i, carry):
        at = rows(i * 208, 208)
        es[at] = e_ref[at].astype(BF16)
        return carry

    lax.fori_loop(0, 32, cast, 0)

    pl.semaphore_wait(barrier, len(peers))

    y_in = {}
    for d in (2, 1, 3):
        to = (y + d) % 4
        src = x_ref.at[:, pl.ds(pl.multiple_of(to * YSEG, 128), YSEG)]
        y_in[d] = put(src, xy.at[d - 1], at_y(d))
    v_far = put(vb.at[:, :, q], vb.at[:, :, q], z_far)
    v_sib = put(vb.at[:, :, q], vb.at[:, :, q], sibling)

    def x_stage(d):
        def piece(zl, to):
            at = zl * SLAB + to * ROWS
            if d == 0:
                return x_ref.at[:, pl.ds(pl.multiple_of(y * YSEG + at, 128), ROWS)]
            return xy.at[d - 1, :, pl.ds(pl.multiple_of(at, 128), ROWS)]

        mine, other = xb.at[d, zlo, x, zhi, k], xs.at[d, x]
        waits = []
        for e in (2, 1, 3):
            to = (x + e) % 4
            waits.append(put(piece(zlo, to), mine, at_x(e)))
            waits.append(put(piece(1 - zlo, to), other, at_x(e)))
        return waits, [move(piece(zlo, x), mine), move(piece(1 - zlo, x), other)]

    own_cols = rows(x * 128, 128)

    def e_stage(half):
        waits = []
        for e in (2, 1, 3):
            src = es.at[rows(((x + e) % 4 * 2 + half) * HALF, HALF)]
            waits.append(put(src, eb.at[half * HALF : (half + 1) * HALF, own_cols], at_x(e)))
        return waits

    def z_stage(d):
        block = xb.at[d, zlo, :, zhi, k]
        return [
            put(block, block, z_far),
            put(xs.at[d], block, z_near),
            put(xs.at[d], block, z_other),
        ]

    x_in, z_in, c_in = {}, {}, {}
    x_in[0] = x_stage(0)
    e_in = e_stage(0)
    e_own = move(es.at[rows(x * ROWS, ROWS)], eb.at[:, own_cols])
    for d in (2, 1, 3):
        y_in[d].wait_recv()
        x_in[d] = x_stage(d)
    order = (2, 1, 3, 0)
    for d in order:
        arrived(x_in[d][0])
        for copy in x_in[d][1]:
            copy.wait()
        z_in[d] = z_stage(d)
        if d == 2:
            e_in += e_stage(1)

    v_far.wait_recv()
    far = (1 - zhi) * 2 + k
    v_pass = put(vb.at[:, :, far], vb.at[:, :, far], sibling)
    v_sib.wait_recv()
    v_pass.wait_recv()

    for term in range(2):
        vq[:, term * 128 : (term + 1) * 128] = vb[term, q].reshape(ROWS, 128)
        vc[:, term * 128 : (term + 1) * 128] = vb[term, k].reshape(ROWS, 128)
        for chunk in range(4):
            vt[term, chunk * 128 : (chunk + 1) * 128, :] = vb[term, chunk].reshape(ROWS, 128).T
    both = mm(vt[0], vc[...])
    vv[...] = both[:, :128] + both[:, 128:] + mm(vt[1], vc[:, :128])
    vv_in = [
        put(vv.at[rows((y - d) % 4 * 128, 128)], rvv.at[d - 1], at_y(-d)) for d in (2, 1, 3)
    ]

    def forward(d):
        arrived(z_in[d])
        block = xb.at[d, :, :, :, k]
        c_in[d] = put(block, block, sibling)

    def project_panel(d):
        c_in[d].wait_recv()

        def pack(i, carry):
            value = xb[d, i // 4, i % 4].astype(F32).reshape(32, ROWS)
            x2[d, rows(i * 32, 32)] = value.astype(BF16)
            return carry

        lax.fori_loop(0, 8, pack, 0)
        both = mm(x2[d], vq[...])
        px[d] = both[:, :128] + both[:, 128:]
        if d > 0:
            return put(px.at[d], rx.at[d - 1], at_y(-d))

    def project(d):
        part = mm(x2[d], eb[...])
        for j in range(4):
            pa[d, j] = part[:128, j * 128 : (j + 1) * 128]
            pb[d, j] = part[128:, j * 128 : (j + 1) * 128]
        if d > 0:
            a_in.append(put(pa.at[d], ra.at[d - 1], at_y(-d)))
        b_in[d] = [put(pb.at[d, (x + e) % 4], rb.at[e - 1, d], at_x(e)) for e in (2, 1, 3)]

    px_in, a_in, b_in = [], [], {}
    forward(2)
    px_in.append(project_panel(2))

    arrived(vv_in)
    svv[...] = vv[rows(y * 128, 128)] + rvv[0] + rvv[1] + rvv[2]
    vvx_in = [put(svv, rvx.at[e - 1], at_x(e)) for e in (2, 1, 3)]

    forward(1)
    px_in.append(project_panel(1))

    arrived(e_in)
    e_own.wait()
    project(2)

    for half in range(2):
        cols = eb[:, half * 256 : (half + 1) * 256]
        part = mm(vt[0], cols) + mm(vt[1], cols)
        for j in range(2):
            for chunk in range(4):
                tile = part[chunk * 128 : (chunk + 1) * 128, j * 128 : (j + 1) * 128]
                va[chunk, 2 * half + j] = tile[:64]
                vbp[2 * half + j, chunk] = tile[64:]
    va_in = [put(va.at[(y - d) % 4], rva.at[d - 1], at_y(-d)) for d in (2, 1, 3)]
    vb_in = [put(vbp.at[(x + e) % 4], rvb.at[e - 1], at_x(e)) for e in (2, 1, 3)]

    project(1)
    forward(3)
    px_in.append(project_panel(3))
    project(3)
    forward(0)
    project_panel(0)
    project(0)

    arrived(px_in)
    sx[...] = px[0] + rx[0] + rx[1] + rx[2]
    xz_in = put(sx.at[rows((1 - zlo) * 128, 128)], rzx, z_near)

    arrived(va_in)
    sva[...] = va[y] + rva[0] + rva[1] + rva[2]
    va2_in = [put(sva.at[(x + e) % 4], rvxa.at[e - 1], at_x(e)) for e in (2, 1, 3)]
    arrived(vb_in)
    svb[...] = vbp[x] + rvb[0] + rvb[1] + rvb[2]
    vb2_in = [put(svb.at[(y - d) % 4], rvyb.at[d - 1], at_y(-d)) for d in (2, 1, 3)]

    xz_in.wait_recv()
    s2x[...] = sx[rows(zlo * 128, 128)] + rzx[...]
    xx_in = [put(s2x, rx2.at[e - 1], at_x(e)) for e in (2, 1, 3)]

    b2_in = []
    for d in order:
        arrived(b_in[d])
        sb[d] = pb[d, x] + rb[0, d] + rb[1, d] + rb[2, d]
        if d > 0:
            b2_in.append(put(sb.at[d], ryb.at[d - 1], at_y(-d)))

    arrived(vvx_in)
    uz[1] = svv[...] + rvx[0] + rvx[1] + rvx[2]
    arrived(va2_in)
    uz[0, :64] = sva[x] + rvxa[0] + rvxa[1] + rvxa[2]
    arrived(vb2_in)
    uz[0, 64:] = svb[y] + rvyb[0] + rvyb[1] + rvyb[2]
    uz_in = put(uz, ruz, z_near)

    arrived(a_in)
    for j in range(4):
        sa[j] = pa[0, j] + ra[0, j] + ra[1, j] + ra[2, j]
    a2_in = [put(sa.at[(x + e) % 4], rxa.at[e - 1], at_x(e)) for e in (2, 1, 3)]

    arrived(xx_in)
    xv[q] = s2x[...] + rx2[0] + rx2[1] + rx2[2]
    far_in = put(xv.at[q], xv.at[q], z_far)
    sib_in = put(xv.at[q], xv.at[q], sibling)

    uz_in.wait_recv()
    own = rows(y * 128, 128)
    u[:, own] = uz[...] + ruz[...]
    uy_in = [put(u.at[:, own], u.at[:, own], at_y(d)) for d in (2, 1, 3)]

    arrived(b2_in)
    ab[1] = sb[0] + ryb[0] + ryb[1] + ryb[2]
    arrived(a2_in)
    ab[0] = sa[x] + rxa[0] + rxa[1] + rxa[2]
    ab_in = put(ab.at[1 - zlo], rab, z_near)

    far_in.wait_recv()
    pass_in = put(xv.at[far], xv.at[far], sibling)

    arrived(uy_in)
    g[k] = u[1, 256:512]
    g_in = put(g.at[k], g.at[k], sibling)
    middle_second = exact(t2_ref[...], u[0, 0:256])
    g_in.wait_recv()
    inner_first = (
        u[0, 256:512] - exact(g[0], middle_second[:128]) - exact(g[1], middle_second[128:])
    )
    middle_first = exact(t1_ref[...], inner_first)

    sib_in.wait_recv()
    pass_in.wait_recv()
    total = jnp.zeros((128, 128), F32)
    for j in range(4):
        middle = middle_second if j < 2 else middle_first
        total += exact(xv[j], middle[(j % 2) * 128 : (j % 2 + 1) * 128])
    ab_in.wait_recv()
    out_ref[...] = (ab[zlo] + rab[...] - total) * lax.rsqrt(ev_ref[...])

    for copy in started:
        copy.wait_send()


def per_device(tokens, eigvecs, eigvals, v_first, v_second, t_first, t_second):
    vmem = pl.BlockSpec(memory_space=pltpu.VMEM)
    return pl.pallas_call(
        kernel,
        out_shape=jax.ShapeDtypeStruct((128, 128), F32),
        in_specs=[vmem] * 7,
        out_specs=vmem,
        scratch_shapes=[
            pltpu.VMEM((3, 8, YSEG), BF16),
            pltpu.VMEM((4, 4, 8, ROWS), BF16),
            pltpu.VMEM((4, 2, 4, 2, 2, 8, ROWS), BF16),
            pltpu.VMEM((4, 256, ROWS), BF16),
            pltpu.VMEM((SLAB, 128), BF16),
            pltpu.VMEM((ROWS, 512), BF16),
            pltpu.VMEM((2, 4, 4, OWN, 128), BF16),
            pltpu.VMEM((2, 512, ROWS), BF16),
            pltpu.VMEM((ROWS, 256), BF16),
            pltpu.VMEM((ROWS, 256), BF16),
            pltpu.VMEM((4, 4, 128, 128), F32),
            pltpu.VMEM((3, 4, 128, 128), F32),
            pltpu.VMEM((4, 128, 128), F32),
            pltpu.VMEM((3, 128, 128), F32),
            pltpu.VMEM((4, 4, 128, 128), F32),
            pltpu.VMEM((3, 4, 128, 128), F32),
            pltpu.VMEM((4, 128, 128), F32),
            pltpu.VMEM((3, 128, 128), F32),
            pltpu.VMEM((2, 128, 128), F32),
            pltpu.VMEM((128, 128), F32),
            pltpu.VMEM((4, 256, 128), F32),
            pltpu.VMEM((3, 256, 128), F32),
            pltpu.VMEM((256, 128), F32),
            pltpu.VMEM((128, 128), F32),
            pltpu.VMEM((128, 128), F32),
            pltpu.VMEM((3, 128, 128), F32),
            pltpu.VMEM((4, 128, 128), F32),
            pltpu.VMEM((4, 4, 64, 128), F32),
            pltpu.VMEM((3, 4, 64, 128), F32),
            pltpu.VMEM((4, 64, 128), F32),
            pltpu.VMEM((3, 64, 128), F32),
            pltpu.VMEM((4, 4, 64, 128), F32),
            pltpu.VMEM((3, 4, 64, 128), F32),
            pltpu.VMEM((4, 64, 128), F32),
            pltpu.VMEM((3, 64, 128), F32),
            pltpu.VMEM((512, 128), F32),
            pltpu.VMEM((3, 128, 128), F32),
            pltpu.VMEM((128, 128), F32),
            pltpu.VMEM((3, 128, 128), F32),
            pltpu.VMEM((2, 128, 128), F32),
            pltpu.VMEM((2, 128, 128), F32),
            pltpu.VMEM((2, 512, 128), F32),
            pltpu.VMEM((2, 256, 128), F32),
            pltpu.SemaphoreType.DMA((COPIES,)),
            pltpu.SemaphoreType.DMA((COPIES,)),
            pltpu.SemaphoreType.DMA((16,)),
        ],
        compiler_params=pltpu.CompilerParams(
            collective_id=0, has_side_effects=True, vmem_limit_bytes=56 * 1024 * 1024
        ),
    )(tokens, eigvecs, v_first, v_second, t_first, t_second, eigvals.reshape(1, 128))


def solution(mesh):
    in_specs = (
        P(("row", "col"), None),
        P("row", "col"),
        P("col"),
        P(("row", "col"), None),
        P(("row", "col"), None),
        P(),
        P(),
    )
    out_specs = P("row", "col")
    return jax.shard_map(
        per_device, mesh=mesh, in_specs=in_specs, out_specs=out_specs, check_vma=False
    )
```

```python
import functools

import jax
import jax.numpy as jnp
from jax import lax
from jax.experimental import pallas as pl
from jax.experimental.pallas import tpu as pltpu
from jax.sharding import PartitionSpec as P

MESH = pl.DeviceIdType.MESH
BF16 = jnp.bfloat16
F32 = jnp.float32
HIGH = lax.Precision.HIGHEST

ROWS = 1664
OWN = 416
SLAB = 6656
YSEG = 2 * SLAB
HALF = ROWS // 2
COPIES = 128


def mm(a, b):
    return jnp.dot(a, b, preferred_element_type=F32)


def exact(a, b):
    return jnp.dot(a, b, precision=HIGH, preferred_element_type=F32)


def kernel(
    x_ref, e_ref, v1_ref, v2_ref, t1_ref, t2_ref, out_ref,
    xy, xs, xb, x2, ef, es, eb, vb, vt, vq, vc,
    pa, ha, ra, sa, rxa, pb, rb, sb, ryb, ab, rab,
    px, hx, rx, sx, rzx, s2x, rx2, xv,
    va, hva, rva, sva, rvxa, vbp, rvb, svb, rvyb, uz, ruz, u,
    vv, rvv, svv, rvx, uv, ruv, g,
    send, recv, local,
):
    r, c = lax.axis_index("row"), lax.axis_index("col")
    y, zlo = r // 2, r % 2
    x, q = c // 4, c % 4
    zhi, k = q // 2, q % 2

    def at_y(d):
        return (((y + d) % 4) * 2 + zlo, c)

    def at_x(d):
        return (r, ((x + d) % 4) * 4 + q)

    z_far = (r, x * 4 + (1 - zhi) * 2 + k)
    z_near = (y * 2 + 1 - zlo, c)
    z_other = (y * 2 + 1 - zlo, x * 4 + (1 - zhi) * 2 + k)
    sibling = (r, x * 4 + zhi * 2 + 1 - k)

    peers = [at_y(1), at_y(2), at_y(3), at_x(1), at_x(2), at_x(3)]
    peers += [z_far, z_near, z_other, sibling]
    barrier = pltpu.get_barrier_semaphore()
    for peer in peers:
        pl.semaphore_signal(barrier, inc=1, device_id=peer, device_id_type=MESH)

    started = []

    def put(src, dst, device):
        slot = len(started)
        copy = pltpu.make_async_remote_copy(
            src_ref=src, dst_ref=dst, send_sem=send.at[slot], recv_sem=recv.at[slot],
            device_id=device, device_id_type=MESH,
        )
        copy.start()
        started.append(copy)
        return copy

    here = []

    def move(src, dst):
        copy = pltpu.make_async_copy(src, dst, local.at[len(here)])
        copy.start()
        here.append(copy)
        return copy

    def arrived(copies):
        for copy in copies:
            copy.wait_recv()

    def rows(start, size):
        return pl.ds(pl.multiple_of(start, size), size)

    loads = [move(e_ref.at[rows(i * ROWS, ROWS)], ef.at[rows(i * ROWS, ROWS)]) for i in range(4)]

    for chunk in range(4):
        panel = v2_ref if chunk < 2 else v1_ref
        value = panel[:, (chunk % 2) * 128 : (chunk % 2 + 1) * 128]
        high = value.astype(BF16)
        vb[0, chunk, q] = high
        vb[1, chunk, q] = (value - high.astype(F32)).astype(BF16)

    pl.semaphore_wait(barrier, len(peers))

    y_in = {}
    for d in (2, 1, 3):
        to = (y + d) % 4
        src = x_ref.at[:, pl.ds(pl.multiple_of(to * YSEG, 128), YSEG)]
        y_in[d] = put(src, xy.at[d - 1], at_y(d))
    v_far = put(vb.at[:, :, q], vb.at[:, :, q], z_far)
    v_sib = put(vb.at[:, :, q], vb.at[:, :, q], sibling)

    def x_stage(d):
        def piece(zl, to):
            at = zl * SLAB + to * ROWS
            if d == 0:
                return x_ref.at[:, pl.ds(pl.multiple_of(y * YSEG + at, 128), ROWS)]
            return xy.at[d - 1, :, pl.ds(pl.multiple_of(at, 128), ROWS)]

        mine, other = xb.at[d, zlo, x, zhi, k], xs.at[d, x]
        waits = []
        for e in (2, 1, 3):
            to = (x + e) % 4
            waits.append(put(piece(zlo, to), mine, at_x(e)))
            waits.append(put(piece(1 - zlo, to), other, at_x(e)))
        return waits, [move(piece(zlo, x), mine), move(piece(1 - zlo, x), other)]

    own_cols = rows(x * 128, 128)

    def e_stage(half):
        waits = []
        for e in (2, 1, 3):
            src = es.at[rows(((x + e) % 4 * 2 + half) * HALF, HALF)]
            waits.append(put(src, eb.at[half * HALF : (half + 1) * HALF, own_cols], at_x(e)))
        return waits

    def z_stage(d):
        block = xb.at[d, zlo, :, zhi, k]
        return [
            put(block, block, z_far),
            put(xs.at[d], block, z_near),
            put(xs.at[d], block, z_other),
        ]

    x_in, z_in, c_in = {}, {}, {}
    x_in[0] = x_stage(0)

    def cast(i, carry):
        at = rows(i * 208, 208)
        es[at] = ef[at].astype(BF16)
        return carry

    def keep(i, carry):
        eb[rows(i * 208, 208), own_cols] = es[rows(x * ROWS + i * 208, 208)]
        return carry

    for copy in loads:
        copy.wait()
    lax.fori_loop(0, 32, cast, 0)
    e_in = e_stage(0)
    lax.fori_loop(0, 8, keep, 0)
    y_in[2].wait_recv()
    x_in[2] = x_stage(2)
    for d in (1, 3):
        y_in[d].wait_recv()
        x_in[d] = x_stage(d)

    def along_z(d):
        arrived(x_in[d][0])
        for copy in x_in[d][1]:
            copy.wait()
        z_in[d] = z_stage(d)

    for d in (2, 1, 3, 0):
        along_z(d)
        if d == 2:
            e_in += e_stage(1)

    def forward(d):
        arrived(z_in[d])
        block = xb.at[d, :, :, :, k]
        c_in[d] = put(block, block, sibling)

    def halves(value, got):
        half = value.shape[0] // 2
        return {
            1: put(value.at[:half], got.at[0], at_y(-1)),
            3: put(value.at[half:], got.at[1], at_y(1)),
        }

    def project_panel(d):
        c_in[d].wait_recv()

        def pack(i, carry):
            value = xb[d, i // 4, i % 4].astype(F32).reshape(32, ROWS)
            x2[d, rows(i * 32, 32)] = value.astype(BF16)
            return carry

        lax.fori_loop(0, 8, pack, 0)
        both = mm(x2[d], vq[...])
        px[d] = both[:, :128] + both[:, 128:]

    def send_panel(d):
        x_half[d].wait_recv()
        if d == 1:
            px[1, :128] += hx[0]
            return put(px.at[1], rx.at[0], at_y(-1))
        px[3, 128:] += hx[1]
        return put(px.at[3], rx.at[1], at_y(1))

    def project(d):
        part = mm(x2[d], eb[...])
        for j in range(4):
            pa[d, j] = part[:128, j * 128 : (j + 1) * 128]
            pb[d, j] = part[128:, j * 128 : (j + 1) * 128]
        b_in[d] = [put(pb.at[d, (x + e) % 4], rb.at[e - 1, d], at_x(e)) for e in (2, 1, 3)]

    def send_lower(d):
        a_half[d].wait_recv()
        if d == 1:
            pa[1, :2] += ha[0]
            return put(pa.at[1], ra.at[0], at_y(-1))
        pa[3, 2:] += ha[1]
        return put(pa.at[3], ra.at[1], at_y(1))

    v_far.wait_recv()
    far = (1 - zhi) * 2 + k
    v_pass = put(vb.at[:, :, far], vb.at[:, :, far], sibling)
    forward(2)
    v_sib.wait_recv()
    v_pass.wait_recv()

    for term in range(2):
        vq[:, term * 128 : (term + 1) * 128] = vb[term, q].reshape(ROWS, 128)
        vc[:, term * 128 : (term + 1) * 128] = vb[term, k].reshape(ROWS, 128)
        for chunk in range(4):
            vt[term, chunk * 128 : (chunk + 1) * 128, :] = vb[term, chunk].reshape(ROWS, 128).T
    block = rows(256 + zhi * 128, 128)
    both = mm(vt[0, block], vc[...])
    vv[...] = both[:, :128] + both[:, 128:] + mm(vt[1, block], vc[:, :128])
    vv_in = [put(vv.at[rows((y - d) % 4 * 32, 32)], rvv.at[d - 1], at_y(-d)) for d in (2, 1, 3)]

    arrived(e_in)
    for half in range(2):
        cols = eb[:, half * 256 : (half + 1) * 256]
        part = mm(vt[0], cols) + mm(vt[1], cols)
        for j in range(2):
            for chunk in range(4):
                tile = part[chunk * 128 : (chunk + 1) * 128, j * 128 : (j + 1) * 128]
                va[chunk, 2 * half + j] = tile[:64]
                vbp[2 * half + j, chunk] = tile[64:]
    v_half = halves(va.at[(y + 2) % 4], hva)
    vb_in = [put(vbp.at[(x + e) % 4], rvb.at[e - 1], at_x(e)) for e in (2, 1, 3)]

    px_in, a_in, b_in = [], [], {}
    forward(1)
    project_panel(2)
    x_half = halves(px.at[2], hx)
    project(2)
    a_half = halves(pa.at[2], ha)

    arrived(vv_in)
    svv[...] = vv[rows(y * 32, 32)] + rvv[0] + rvv[1] + rvv[2]
    vvx_in = [put(svv, rvx.at[e - 1], at_x(e)) for e in (2, 1, 3)]

    project_panel(1)
    forward(3)
    project(1)
    px_in.append(send_panel(1))

    v_half[1].wait_recv()
    va[(y + 3) % 4, :2] += hva[0]
    va_in = [put(va.at[(y + 3) % 4], rva.at[0], at_y(-1))]
    v_half[3].wait_recv()
    va[(y + 1) % 4, 2:] += hva[1]
    va_in.append(put(va.at[(y + 1) % 4], rva.at[1], at_y(1)))

    a_in.append(send_lower(1))

    project_panel(3)
    px_in.append(send_panel(3))
    forward(0)
    project(3)
    a_in.append(send_lower(3))

    arrived(vvx_in)
    uv[...] = svv[...] + rvx[0] + rvx[1] + rvx[2]
    uv_in = put(uv, ruv, z_near)

    project_panel(0)
    project(0)

    arrived(va_in)
    sva[...] = va[y] + rva[0] + rva[1]
    va2_in = [put(sva.at[(x + e) % 4], rvxa.at[e - 1], at_x(e)) for e in (2, 1, 3)]
    arrived(vb_in)
    svb[...] = vbp[x] + rvb[0] + rvb[1] + rvb[2]
    vb2_in = [put(svb.at[(y - d) % 4], rvyb.at[d - 1], at_y(-d)) for d in (2, 1, 3)]

    arrived(px_in)
    sx[...] = px[0] + rx[0] + rx[1]
    xz_in = put(sx.at[rows((1 - zlo) * 128, 128)], rzx, z_near)

    own = rows(y * 32, 32)
    uv_in.wait_recv()
    g[zhi, k, own] = uv[...] + ruv[...]
    gy_in = [put(g.at[zhi, k, own], g.at[zhi, k, own], at_y(d)) for d in (2, 1, 3)]

    b2_in = []
    for d in (2, 1, 3):
        arrived(b_in[d])
        sb[d] = pb[d, x] + rb[0, d] + rb[1, d] + rb[2, d]
        b2_in.append(put(sb.at[d], ryb.at[d - 1], at_y(-d)))

    xz_in.wait_recv()
    s2x[...] = sx[rows(zlo * 128, 128)] + rzx[...]
    xx_in = [put(s2x, rx2.at[e - 1], at_x(e)) for e in (2, 1, 3)]

    arrived(a_in)
    for j in range(4):
        sa[j] = pa[0, j] + ra[0, j] + ra[1, j]
    a2_in = [put(sa.at[(x + e) % 4], rxa.at[e - 1], at_x(e)) for e in (2, 1, 3)]

    arrived(va2_in)
    uz[:64] = sva[x] + rvxa[0] + rvxa[1] + rvxa[2]
    arrived(vb2_in)
    uz[64:] = svb[y] + rvyb[0] + rvyb[1] + rvyb[2]
    uz_in = put(uz, ruz, z_near)

    arrived(gy_in)
    g_far = put(g.at[zhi, k], g.at[zhi, k], z_far)
    g_sib = put(g.at[zhi, k], g.at[zhi, k], sibling)

    arrived(xx_in)
    xv[q] = s2x[...] + rx2[0] + rx2[1] + rx2[2]
    far_in = put(xv.at[q], xv.at[q], z_far)
    sib_in = put(xv.at[q], xv.at[q], sibling)

    uz_in.wait_recv()
    own = rows(y * 128, 128)
    u[own] = uz[...] + ruz[...]
    uy_in = [put(u.at[own], u.at[own], at_y(d)) for d in (2, 1, 3)]

    g_far.wait_recv()
    g_pass = put(g.at[1 - zhi, k], g.at[1 - zhi, k], sibling)

    arrived(b_in[0])
    arrived(b2_in)
    ab[1] = pb[0, x] + rb[0, 0] + rb[1, 0] + rb[2, 0] + ryb[0] + ryb[1] + ryb[2]

    arrived(a2_in)
    ab[0] = sa[x] + rxa[0] + rxa[1] + rxa[2]
    ab_in = put(ab.at[1 - zlo], rab, z_near)

    far_in.wait_recv()
    pass_in = put(xv.at[far], xv.at[far], sibling)

    arrived(uy_in)
    middle_second = exact(t2_ref[...], u[0:256])
    g_sib.wait_recv()
    g_pass.wait_recv()
    lower, upper = middle_second[:128], middle_second[128:]
    inner_first = u[256:512] - jnp.concatenate(
        [exact(g[i, 0], lower) + exact(g[i, 1], upper) for i in range(2)], axis=0
    )
    middle_first = exact(t1_ref[...], inner_first)

    sib_in.wait_recv()
    pass_in.wait_recv()
    total = jnp.zeros((128, 128), F32)
    for j in range(4):
        middle = middle_second if j < 2 else middle_first
        total += exact(xv[j], middle[(j % 2) * 128 : (j % 2 + 1) * 128])
    ab_in.wait_recv()
    out_ref[...] = ab[zlo] + rab[...] - total

    for copy in started:
        copy.wait_send()


def per_device(tokens, eigvecs, eigvals, v_first, v_second, t_first, t_second):
    vmem = pl.BlockSpec(memory_space=pltpu.VMEM)
    hbm = pl.BlockSpec(memory_space=pltpu.HBM)
    projected = pl.pallas_call(
        kernel,
        out_shape=jax.ShapeDtypeStruct((128, 128), F32),
        in_specs=[hbm, hbm] + [vmem] * 4,
        out_specs=vmem,
        scratch_shapes=[
            pltpu.VMEM((3, 8, YSEG), BF16),
            pltpu.VMEM((4, 4, 8, ROWS), BF16),
            pltpu.VMEM((4, 2, 4, 2, 2, 8, ROWS), BF16),
            pltpu.VMEM((4, 256, ROWS), BF16),
            pltpu.VMEM((SLAB, 128), F32),
            pltpu.VMEM((SLAB, 128), BF16),
            pltpu.VMEM((ROWS, 512), BF16),
            pltpu.VMEM((2, 4, 4, OWN, 128), BF16),
            pltpu.VMEM((2, 512, ROWS), BF16),
            pltpu.VMEM((ROWS, 256), BF16),
            pltpu.VMEM((ROWS, 256), BF16),
            pltpu.VMEM((4, 4, 128, 128), F32),
            pltpu.VMEM((2, 2, 128, 128), F32),
            pltpu.VMEM((2, 4, 128, 128), F32),
            pltpu.VMEM((4, 128, 128), F32),
            pltpu.VMEM((3, 128, 128), F32),
            pltpu.VMEM((4, 4, 128, 128), F32),
            pltpu.VMEM((3, 4, 128, 128), F32),
            pltpu.VMEM((4, 128, 128), F32),
            pltpu.VMEM((3, 128, 128), F32),
            pltpu.VMEM((2, 128, 128), F32),
            pltpu.VMEM((128, 128), F32),
            pltpu.VMEM((4, 256, 128), F32),
            pltpu.VMEM((2, 128, 128), F32),
            pltpu.VMEM((2, 256, 128), F32),
            pltpu.VMEM((256, 128), F32),
            pltpu.VMEM((128, 128), F32),
            pltpu.VMEM((128, 128), F32),
            pltpu.VMEM((3, 128, 128), F32),
            pltpu.VMEM((4, 128, 128), F32),
            pltpu.VMEM((4, 4, 64, 128), F32),
            pltpu.VMEM((2, 2, 64, 128), F32),
            pltpu.VMEM((2, 4, 64, 128), F32),
            pltpu.VMEM((4, 64, 128), F32),
            pltpu.VMEM((3, 64, 128), F32),
            pltpu.VMEM((4, 4, 64, 128), F32),
            pltpu.VMEM((3, 4, 64, 128), F32),
            pltpu.VMEM((4, 64, 128), F32),
            pltpu.VMEM((3, 64, 128), F32),
            pltpu.VMEM((128, 128), F32),
            pltpu.VMEM((128, 128), F32),
            pltpu.VMEM((512, 128), F32),
            pltpu.VMEM((128, 128), F32),
            pltpu.VMEM((3, 32, 128), F32),
            pltpu.VMEM((32, 128), F32),
            pltpu.VMEM((3, 32, 128), F32),
            pltpu.VMEM((32, 128), F32),
            pltpu.VMEM((32, 128), F32),
            pltpu.VMEM((2, 2, 128, 128), F32),
            pltpu.SemaphoreType.DMA((COPIES,)),
            pltpu.SemaphoreType.DMA((COPIES,)),
            pltpu.SemaphoreType.DMA((16,)),
        ],
        compiler_params=pltpu.CompilerParams(
            collective_id=0, has_side_effects=True, vmem_limit_bytes=56 * 1024 * 1024
        ),
    )(tokens, eigvecs, v_first, v_second, t_first, t_second)
    return projected * lax.rsqrt(eigvals)[None, :]


def solution(mesh):
    in_specs = (
        P(("row", "col"), None),
        P("row", "col"),
        P("col"),
        P(("row", "col"), None),
        P(("row", "col"), None),
        P(),
        P(),
    )
    out_specs = P("row", "col")
    return jax.shard_map(
        per_device, mesh=mesh, in_specs=in_specs, out_specs=out_specs, check_vma=False
    )
```

```python
import functools

import jax
import jax.numpy as jnp
from jax import lax
from jax.experimental import pallas as pl
from jax.experimental.pallas import tpu as pltpu
from jax.sharding import PartitionSpec as P

MESH = pl.DeviceIdType.MESH
BF16 = jnp.bfloat16
F32 = jnp.float32
HIGH = lax.Precision.HIGHEST

ROWS = 1664
OWN = 416
SLAB = 6656
YSEG = 2 * SLAB
HALF = ROWS // 2
COPIES = 128


def mm(a, b):
    return jnp.dot(a, b, preferred_element_type=F32)


def exact(a, b):
    return jnp.dot(a, b, precision=HIGH, preferred_element_type=F32)


def kernel(
    x_ref, e_ref, v1_ref, v2_ref, t1_ref, t2_ref, out_ref,
    xy, xs, xb, x2, ef, es, eb, vb, vt, vq, vc,
    pa, ha, ra, sa, rxa, pb, rb, sb, ryb, ab, rab,
    px, hx, rx, sx, rzx, s2x, rx2, xv,
    va, hva, rva, sva, rvxa, vbp, rvb, svb, rvyb, uz, ruz, u,
    vv, rvv, svv, rvx, uv, ruv, g,
    send, recv, local,
):
    r, c = lax.axis_index("row"), lax.axis_index("col")
    y, zlo = r // 2, r % 2
    x, q = c // 4, c % 4
    zhi, k = q // 2, q % 2

    def at_y(d):
        return (((y + d) % 4) * 2 + zlo, c)

    def at_x(d):
        return (r, ((x + d) % 4) * 4 + q)

    z_far = (r, x * 4 + (1 - zhi) * 2 + k)
    z_near = (y * 2 + 1 - zlo, c)
    z_other = (y * 2 + 1 - zlo, x * 4 + (1 - zhi) * 2 + k)
    sibling = (r, x * 4 + zhi * 2 + 1 - k)

    peers = [at_y(1), at_y(2), at_y(3), at_x(1), at_x(2), at_x(3)]
    peers += [z_far, z_near, z_other, sibling]
    barrier = pltpu.get_barrier_semaphore()
    for peer in peers:
        pl.semaphore_signal(barrier, inc=1, device_id=peer, device_id_type=MESH)

    started = []

    def put(src, dst, device):
        slot = len(started)
        copy = pltpu.make_async_remote_copy(
            src_ref=src, dst_ref=dst, send_sem=send.at[slot], recv_sem=recv.at[slot],
            device_id=device, device_id_type=MESH,
        )
        copy.start()
        started.append(copy)
        return copy

    here = []

    def move(src, dst):
        copy = pltpu.make_async_copy(src, dst, local.at[len(here)])
        copy.start()
        here.append(copy)
        return copy

    def arrived(copies):
        for copy in copies:
            copy.wait_recv()

    def rows(start, size):
        return pl.ds(pl.multiple_of(start, size), size)

    loads = [move(e_ref.at[rows(i * ROWS, ROWS)], ef.at[rows(i * ROWS, ROWS)]) for i in range(4)]

    for chunk in range(4):
        panel = v2_ref if chunk < 2 else v1_ref
        value = panel[:, (chunk % 2) * 128 : (chunk % 2 + 1) * 128]
        high = value.astype(BF16)
        vb[0, chunk, q] = high
        vb[1, chunk, q] = (value - high.astype(F32)).astype(BF16)

    pl.semaphore_wait(barrier, len(peers))

    y_in = {}
    for d in (2, 1, 3):
        to = (y + d) % 4
        src = x_ref.at[:, pl.ds(pl.multiple_of(to * YSEG, 128), YSEG)]
        y_in[d] = put(src, xy.at[d - 1], at_y(d))
    v_far = put(vb.at[:, :, q], vb.at[:, :, q], z_far)
    v_sib = put(vb.at[:, :, q], vb.at[:, :, q], sibling)

    def x_stage(d):
        def piece(zl, to):
            at = zl * SLAB + to * ROWS
            if d == 0:
                return x_ref.at[:, pl.ds(pl.multiple_of(y * YSEG + at, 128), ROWS)]
            return xy.at[d - 1, :, pl.ds(pl.multiple_of(at, 128), ROWS)]

        mine, other = xb.at[d, zlo, x, zhi, k], xs.at[d, x]
        waits = []
        for e in (2, 1, 3):
            to = (x + e) % 4
            waits.append(put(piece(zlo, to), mine, at_x(e)))
            waits.append(put(piece(1 - zlo, to), other, at_x(e)))
        return waits, [move(piece(zlo, x), mine), move(piece(1 - zlo, x), other)]

    own_cols = rows(x * 128, 128)

    def e_stage(half):
        waits = []
        for e in (2, 1, 3):
            src = es.at[rows(((x + e) % 4 * 2 + half) * HALF, HALF)]
            waits.append(put(src, eb.at[half * HALF : (half + 1) * HALF, own_cols], at_x(e)))
        return waits

    def z_stage(d):
        block = xb.at[d, zlo, :, zhi, k]
        return [
            put(block, block, z_far),
            put(xs.at[d], block, z_near),
            put(xs.at[d], block, z_other),
        ]

    x_in, z_in, c_in = {}, {}, {}
    x_in[0] = x_stage(0)

    def cast(i, carry):
        at = rows(i * 208, 208)
        es[at] = ef[at].astype(BF16)
        return carry

    def keep(i, carry):
        eb[rows(i * 208, 208), own_cols] = es[rows(x * ROWS + i * 208, 208)]
        return carry

    for copy in loads:
        copy.wait()
    lax.fori_loop(0, 32, cast, 0)
    e_in = e_stage(0)
    lax.fori_loop(0, 8, keep, 0)
    y_in[2].wait_recv()
    x_in[2] = x_stage(2)
    for d in (1, 3):
        y_in[d].wait_recv()
        x_in[d] = x_stage(d)

    def along_z(d):
        arrived(x_in[d][0])
        for copy in x_in[d][1]:
            copy.wait()
        z_in[d] = z_stage(d)

    for d in (2, 1, 3, 0):
        along_z(d)
        if d == 2:
            e_in += e_stage(1)

    def forward(d):
        arrived(z_in[d])
        block = xb.at[d, :, :, :, k]
        c_in[d] = put(block, block, sibling)

    def halves(value, got):
        half = value.shape[0] // 2
        return {
            1: put(value.at[:half], got.at[0], at_y(-1)),
            3: put(value.at[half:], got.at[1], at_y(1)),
        }

    def project_panel(d):
        c_in[d].wait_recv()

        def pack(i, carry):
            value = xb[d, i // 4, i % 4].astype(F32).reshape(32, ROWS)
            x2[d, rows(i * 32, 32)] = value.astype(BF16)
            return carry

        lax.fori_loop(0, 8, pack, 0)
        both = mm(x2[d], vq[...])
        px[d] = both[:, :128] + both[:, 128:]

    def send_panel(d):
        x_half[d].wait_recv()
        if d == 1:
            px[1, :128] += hx[0]
            return put(px.at[1], rx.at[0], at_y(-1))
        px[3, 128:] += hx[1]
        return put(px.at[3], rx.at[1], at_y(1))

    def project(d):
        part = mm(x2[d], eb[...])
        for j in range(4):
            pa[d, j] = part[:128, j * 128 : (j + 1) * 128]
            pb[d, j] = part[128:, j * 128 : (j + 1) * 128]
        b_in[d] = [put(pb.at[d, (x + e) % 4], rb.at[e - 1, d], at_x(e)) for e in (2, 1, 3)]

    def send_lower(d):
        a_half[d].wait_recv()
        if d == 1:
            pa[1, :2] += ha[0]
            return put(pa.at[1], ra.at[0], at_y(-1))
        pa[3, 2:] += ha[1]
        return put(pa.at[3], ra.at[1], at_y(1))

    v_far.wait_recv()
    far = (1 - zhi) * 2 + k
    v_pass = put(vb.at[:, :, far], vb.at[:, :, far], sibling)
    forward(2)
    v_sib.wait_recv()
    v_pass.wait_recv()

    for term in range(2):
        vq[:, term * 128 : (term + 1) * 128] = vb[term, q].reshape(ROWS, 128)
        vc[:, term * 128 : (term + 1) * 128] = vb[term, k].reshape(ROWS, 128)
        for chunk in range(4):
            vt[term, chunk * 128 : (chunk + 1) * 128, :] = vb[term, chunk].reshape(ROWS, 128).T
    block = rows(256 + zhi * 128, 128)
    both = mm(vt[0, block], vc[...])
    vv[...] = both[:, :128] + both[:, 128:] + mm(vt[1, block], vc[:, :128])
    vv_in = [put(vv.at[rows((y - d) % 4 * 32, 32)], rvv.at[d - 1], at_y(-d)) for d in (2, 1, 3)]

    arrived(e_in)
    for half in range(2):
        cols = eb[:, half * 256 : (half + 1) * 256]
        part = mm(vt[0], cols) + mm(vt[1], cols)
        for j in range(2):
            for chunk in range(4):
                tile = part[chunk * 128 : (chunk + 1) * 128, j * 128 : (j + 1) * 128]
                va[chunk, 2 * half + j] = tile[:64]
                vbp[2 * half + j, chunk] = tile[64:]
    v_half = halves(va.at[(y + 2) % 4], hva)
    vb_in = [put(vbp.at[(x + e) % 4], rvb.at[e - 1], at_x(e)) for e in (2, 1, 3)]


    px_in, a_in, b_in = [], [], {}

    forward(1)

    project_panel(2)
    x_half = halves(px.at[2], hx)

    project(2)
    a_half = halves(pa.at[2], ha)

    arrived(vv_in)
    svv[...] = vv[rows(y * 32, 32)] + rvv[0] + rvv[1] + rvv[2]
    vvx_in = [put(svv, rvx.at[e - 1], at_x(e)) for e in (2, 1, 3)]

    project_panel(1)

    forward(3)

    project(1)

    px_in.append(send_panel(1))

    v_half[1].wait_recv()
    va[(y + 3) % 4, :2] += hva[0]
    va_in = [put(va.at[(y + 3) % 4], rva.at[0], at_y(-1))]
    v_half[3].wait_recv()
    va[(y + 1) % 4, 2:] += hva[1]
    va_in.append(put(va.at[(y + 1) % 4], rva.at[1], at_y(1)))

    a_in.append(send_lower(1))

    project_panel(3)

    px_in.append(send_panel(3))

    forward(0)

    project(3)

    a_in.append(send_lower(3))

    arrived(vvx_in)
    uv[...] = svv[...] + rvx[0] + rvx[1] + rvx[2]
    uv_in = put(uv, ruv, z_near)

    project_panel(0)

    arrived(va_in)
    sva[...] = va[y] + rva[0] + rva[1]
    va2_in = [put(sva.at[(x + e) % 4], rvxa.at[e - 1], at_x(e)) for e in (2, 1, 3)]
    arrived(vb_in)
    svb[...] = vbp[x] + rvb[0] + rvb[1] + rvb[2]
    vb2_in = [put(svb.at[(y - d) % 4], rvyb.at[d - 1], at_y(-d)) for d in (2, 1, 3)]

    project(0)

    arrived(px_in)
    sx[...] = px[0] + rx[0] + rx[1]
    xz_in = put(sx.at[rows((1 - zlo) * 128, 128)], rzx, z_near)

    own = rows(y * 32, 32)
    uv_in.wait_recv()
    g[zhi, k, own] = uv[...] + ruv[...]
    gy_in = [put(g.at[zhi, k, own], g.at[zhi, k, own], at_y(d)) for d in (2, 1, 3)]

    b2_in = []
    for d in (2, 1, 3):
        arrived(b_in[d])
        sb[d] = pb[d, x] + rb[0, d] + rb[1, d] + rb[2, d]
        b2_in.append(put(sb.at[d], ryb.at[d - 1], at_y(-d)))

    xz_in.wait_recv()
    s2x[...] = sx[rows(zlo * 128, 128)] + rzx[...]
    xx_in = [put(s2x, rx2.at[e - 1], at_x(e)) for e in (2, 1, 3)]

    arrived(a_in)
    for j in range(4):
        sa[j] = pa[0, j] + ra[0, j] + ra[1, j]
    a2_in = [put(sa.at[(x + e) % 4], rxa.at[e - 1], at_x(e)) for e in (2, 1, 3)]

    arrived(va2_in)
    uz[:64] = sva[x] + rvxa[0] + rvxa[1] + rvxa[2]
    arrived(vb2_in)
    uz[64:] = svb[y] + rvyb[0] + rvyb[1] + rvyb[2]
    uz_in = put(uz, ruz, z_near)

    arrived(gy_in)
    g_far = put(g.at[zhi, k], g.at[zhi, k], z_far)
    g_sib = put(g.at[zhi, k], g.at[zhi, k], sibling)

    arrived(xx_in)
    xv[q] = s2x[...] + rx2[0] + rx2[1] + rx2[2]
    far_in = put(xv.at[q], xv.at[q], z_far)
    sib_in = put(xv.at[q], xv.at[q], sibling)

    uz_in.wait_recv()
    own = rows(y * 128, 128)
    u[own] = uz[...] + ruz[...]
    uy_in = [put(u.at[own], u.at[own], at_y(d)) for d in (2, 1, 3)]

    g_far.wait_recv()
    g_pass = put(g.at[1 - zhi, k], g.at[1 - zhi, k], sibling)

    arrived(b_in[0])
    arrived(b2_in)
    ab[1] = pb[0, x] + rb[0, 0] + rb[1, 0] + rb[2, 0] + ryb[0] + ryb[1] + ryb[2]

    arrived(a2_in)
    ab[0] = sa[x] + rxa[0] + rxa[1] + rxa[2]
    ab_in = put(ab.at[1 - zlo], rab, z_near)

    far_in.wait_recv()
    pass_in = put(xv.at[far], xv.at[far], sibling)

    arrived(uy_in)
    middle_second = exact(t2_ref[...], u[0:256])
    g_sib.wait_recv()
    g_pass.wait_recv()
    lower, upper = middle_second[:128], middle_second[128:]
    inner_first = u[256:512] - jnp.concatenate(
        [exact(g[i, 0], lower) + exact(g[i, 1], upper) for i in range(2)], axis=0
    )
    middle_first = exact(t1_ref[...], inner_first)

    sib_in.wait_recv()
    pass_in.wait_recv()
    total = jnp.zeros((128, 128), F32)
    for j in range(4):
        middle = middle_second if j < 2 else middle_first
        total += exact(xv[j], middle[(j % 2) * 128 : (j % 2 + 1) * 128])
    ab_in.wait_recv()
    out_ref[...] = ab[zlo] + rab[...] - total

    for copy in started:
        copy.wait_send()


def per_device(tokens, eigvecs, eigvals, v_first, v_second, t_first, t_second):
    vmem = pl.BlockSpec(memory_space=pltpu.VMEM)
    hbm = pl.BlockSpec(memory_space=pltpu.HBM)
    projected = pl.pallas_call(
        kernel,
        out_shape=jax.ShapeDtypeStruct((128, 128), F32),
        in_specs=[hbm, hbm] + [vmem] * 4,
        out_specs=vmem,
        scratch_shapes=[
            pltpu.VMEM((3, 8, YSEG), BF16),
            pltpu.VMEM((4, 4, 8, ROWS), BF16),
            pltpu.VMEM((4, 2, 4, 2, 2, 8, ROWS), BF16),
            pltpu.VMEM((4, 256, ROWS), BF16),
            pltpu.VMEM((SLAB, 128), F32),
            pltpu.VMEM((SLAB, 128), BF16),
            pltpu.VMEM((ROWS, 512), BF16),
            pltpu.VMEM((2, 4, 4, OWN, 128), BF16),
            pltpu.VMEM((2, 512, ROWS), BF16),
            pltpu.VMEM((ROWS, 256), BF16),
            pltpu.VMEM((ROWS, 256), BF16),
            pltpu.VMEM((4, 4, 128, 128), F32),
            pltpu.VMEM((2, 2, 128, 128), F32),
            pltpu.VMEM((2, 4, 128, 128), F32),
            pltpu.VMEM((4, 128, 128), F32),
            pltpu.VMEM((3, 128, 128), F32),
            pltpu.VMEM((4, 4, 128, 128), F32),
            pltpu.VMEM((3, 4, 128, 128), F32),
            pltpu.VMEM((4, 128, 128), F32),
            pltpu.VMEM((3, 128, 128), F32),
            pltpu.VMEM((2, 128, 128), F32),
            pltpu.VMEM((128, 128), F32),
            pltpu.VMEM((4, 256, 128), F32),
            pltpu.VMEM((2, 128, 128), F32),
            pltpu.VMEM((2, 256, 128), F32),
            pltpu.VMEM((256, 128), F32),
            pltpu.VMEM((128, 128), F32),
            pltpu.VMEM((128, 128), F32),
            pltpu.VMEM((3, 128, 128), F32),
            pltpu.VMEM((4, 128, 128), F32),
            pltpu.VMEM((4, 4, 64, 128), F32),
            pltpu.VMEM((2, 2, 64, 128), F32),
            pltpu.VMEM((2, 4, 64, 128), F32),
            pltpu.VMEM((4, 64, 128), F32),
            pltpu.VMEM((3, 64, 128), F32),
            pltpu.VMEM((4, 4, 64, 128), F32),
            pltpu.VMEM((3, 4, 64, 128), F32),
            pltpu.VMEM((4, 64, 128), F32),
            pltpu.VMEM((3, 64, 128), F32),
            pltpu.VMEM((128, 128), F32),
            pltpu.VMEM((128, 128), F32),
            pltpu.VMEM((512, 128), F32),
            pltpu.VMEM((128, 128), F32),
            pltpu.VMEM((3, 32, 128), F32),
            pltpu.VMEM((32, 128), F32),
            pltpu.VMEM((3, 32, 128), F32),
            pltpu.VMEM((32, 128), F32),
            pltpu.VMEM((32, 128), F32),
            pltpu.VMEM((2, 2, 128, 128), F32),
            pltpu.SemaphoreType.DMA((COPIES,)),
            pltpu.SemaphoreType.DMA((COPIES,)),
            pltpu.SemaphoreType.DMA((16,)),
        ],
        compiler_params=pltpu.CompilerParams(
            collective_id=0, has_side_effects=True, vmem_limit_bytes=56 * 1024 * 1024
        ),
    )(tokens, eigvecs, v_first, v_second, t_first, t_second)
    return projected * lax.rsqrt(eigvals)[None, :]


def solution(mesh):
    in_specs = (
        P(("row", "col"), None),
        P("row", "col"),
        P("col"),
        P(("row", "col"), None),
        P(("row", "col"), None),
        P(),
        P(),
    )
    out_specs = P("row", "col")
    return jax.shard_map(
        per_device, mesh=mesh, in_specs=in_specs, out_specs=out_specs, check_vma=False
    )
```

```python
import functools

import jax
import jax.numpy as jnp
from jax import lax
from jax.experimental import pallas as pl
from jax.experimental.pallas import tpu as pltpu
from jax.sharding import PartitionSpec as P

MESH = pl.DeviceIdType.MESH
BF16 = jnp.bfloat16
F32 = jnp.float32
HIGH = lax.Precision.HIGHEST

ROWS = 1664
OWN = 416
SLAB = 6656
YSEG = 2 * SLAB
HALF = ROWS // 2
COPIES = 128


def mm(a, b):
    return jnp.dot(a, b, preferred_element_type=F32)


def exact(a, b):
    return jnp.dot(a, b, precision=HIGH, preferred_element_type=F32)


def kernel(
    x_ref, e_ref, v1_ref, v2_ref, t1_ref, t2_ref, out_ref,
    xy, xs, xb, x2, ef, es, eb, vb, vt, vq, vc,
    pa, ha, ra, sa, rxa, pb, rb, sb, ryb, ab, rab,
    px, hx, rx, sx, rzx, s2x, rx2, xv,
    va, hva, rva, sva, rvxa, vbp, rvb, svb, rvyb, uz, ruz, u,
    vv, rvv, svv, rvx, uv, ruv, g,
    send, recv, local,
):
    r, c = lax.axis_index("row"), lax.axis_index("col")
    y, zlo = r // 2, r % 2
    x, q = c // 4, c % 4
    zhi, k = q // 2, q % 2

    def at_y(d):
        return (((y + d) % 4) * 2 + zlo, c)

    def at_x(d):
        return (r, ((x + d) % 4) * 4 + q)

    z_far = (r, x * 4 + (1 - zhi) * 2 + k)
    z_near = (y * 2 + 1 - zlo, c)
    z_other = (y * 2 + 1 - zlo, x * 4 + (1 - zhi) * 2 + k)
    sibling = (r, x * 4 + zhi * 2 + 1 - k)

    peers = [at_y(1), at_y(2), at_y(3), at_x(1), at_x(2), at_x(3)]
    peers += [z_far, z_near, z_other, sibling]
    barrier = pltpu.get_barrier_semaphore()
    for peer in peers:
        pl.semaphore_signal(barrier, inc=1, device_id=peer, device_id_type=MESH)

    started = []

    def put(src, dst, device):
        slot = len(started)
        copy = pltpu.make_async_remote_copy(
            src_ref=src, dst_ref=dst, send_sem=send.at[slot], recv_sem=recv.at[slot],
            device_id=device, device_id_type=MESH,
        )
        copy.start()
        started.append(copy)
        return copy

    here = []

    def move(src, dst):
        copy = pltpu.make_async_copy(src, dst, local.at[len(here)])
        copy.start()
        here.append(copy)
        return copy

    def arrived(copies):
        for copy in copies:
            copy.wait_recv()

    def rows(start, size):
        return pl.ds(pl.multiple_of(start, size), size)

    loads = [move(e_ref.at[rows(i * ROWS, ROWS)], ef.at[rows(i * ROWS, ROWS)]) for i in range(4)]

    for chunk in range(4):
        panel = v2_ref if chunk < 2 else v1_ref
        value = panel[:, (chunk % 2) * 128 : (chunk % 2 + 1) * 128]
        high = value.astype(BF16)
        vb[0, chunk, q] = high
        vb[1, chunk, q] = (value - high.astype(F32)).astype(BF16)

    pl.semaphore_wait(barrier, len(peers))

    y_in = {}
    for d in (2, 1, 3):
        to = (y + d) % 4
        src = x_ref.at[:, pl.ds(pl.multiple_of(to * YSEG, 128), YSEG)]
        y_in[d] = put(src, xy.at[d - 1], at_y(d))
    v_far = put(vb.at[:, :, q], vb.at[:, :, q], z_far)
    v_sib = put(vb.at[:, :, q], vb.at[:, :, q], sibling)

    def x_stage(d):
        def piece(zl, to):
            at = zl * SLAB + to * ROWS
            if d == 0:
                return x_ref.at[:, pl.ds(pl.multiple_of(y * YSEG + at, 128), ROWS)]
            return xy.at[d - 1, :, pl.ds(pl.multiple_of(at, 128), ROWS)]

        mine, other = xb.at[d, zlo, x, zhi, k], xs.at[d, x]
        waits = []
        for e in (2, 1, 3):
            to = (x + e) % 4
            waits.append(put(piece(zlo, to), mine, at_x(e)))
            waits.append(put(piece(1 - zlo, to), other, at_x(e)))
        return waits, [move(piece(zlo, x), mine), move(piece(1 - zlo, x), other)]

    own_cols = rows(x * 128, 128)

    def e_stage(half):
        waits = []
        for e in (2, 1, 3):
            src = es.at[rows(((x + e) % 4 * 2 + half) * HALF, HALF)]
            waits.append(put(src, eb.at[half * HALF : (half + 1) * HALF, own_cols], at_x(e)))
        return waits

    def z_stage(d):
        block = xb.at[d, zlo, :, zhi, k]
        return [
            put(block, block, z_far),
            put(xs.at[d], block, z_near),
            put(xs.at[d], block, z_other),
        ]

    x_in, z_in, c_in = {}, {}, {}
    x_in[0] = x_stage(0)

    def cast(i, carry):
        at = rows(i * 208, 208)
        es[at] = ef[at].astype(BF16)
        return carry

    def keep(i, carry):
        eb[rows(i * 208, 208), own_cols] = es[rows(x * ROWS + i * 208, 208)]
        return carry

    for copy in loads:
        copy.wait()
    lax.fori_loop(0, 32, cast, 0)
    e_in = e_stage(0)
    lax.fori_loop(0, 8, keep, 0)
    y_in[2].wait_recv()
    x_in[2] = x_stage(2)
    for d in (1, 3):
        y_in[d].wait_recv()
        x_in[d] = x_stage(d)

    def along_z(d):
        arrived(x_in[d][0])
        for copy in x_in[d][1]:
            copy.wait()
        z_in[d] = z_stage(d)

    for d in (2, 1, 3, 0):
        along_z(d)
        if d == 2:
            e_in += e_stage(1)

    def forward(d):
        arrived(z_in[d])
        block = xb.at[d, :, :, :, k]
        c_in[d] = put(block, block, sibling)

    def halves(value, got):
        half = value.shape[0] // 2
        return {
            1: put(value.at[:half], got.at[0], at_y(-1)),
            3: put(value.at[half:], got.at[1], at_y(1)),
        }

    def project_panel(d):
        c_in[d].wait_recv()

        def pack(i, carry):
            value = xb[d, i // 4, i % 4].astype(F32).reshape(32, ROWS)
            x2[d, rows(i * 32, 32)] = value.astype(BF16)
            return carry

        lax.fori_loop(0, 8, pack, 0)
        both = mm(x2[d], vq[...])
        px[d] = both[:, :128] + both[:, 128:]

    def send_panel(d):
        x_half[d].wait_recv()
        if d == 1:
            px[1, :128] += hx[0]
            return put(px.at[1], rx.at[0], at_y(-1))
        px[3, 128:] += hx[1]
        return put(px.at[3], rx.at[1], at_y(1))

    def project(d):
        part = mm(x2[d], eb[...])
        for j in range(4):
            pa[d, j] = part[:128, j * 128 : (j + 1) * 128]
            pb[d, j] = part[128:, j * 128 : (j + 1) * 128]
        b_in[d] = [put(pb.at[d, (x + e) % 4], rb.at[e - 1, d], at_x(e)) for e in (2, 1, 3)]

    def send_lower(d):
        a_half[d].wait_recv()
        if d == 1:
            pa[1, :2] += ha[0]
            return put(pa.at[1], ra.at[0], at_y(-1))
        pa[3, 2:] += ha[1]
        return put(pa.at[3], ra.at[1], at_y(1))

    v_far.wait_recv()
    far = (1 - zhi) * 2 + k
    v_pass = put(vb.at[:, :, far], vb.at[:, :, far], sibling)
    forward(2)
    v_sib.wait_recv()
    v_pass.wait_recv()

    for term in range(2):
        vq[:, term * 128 : (term + 1) * 128] = vb[term, q].reshape(ROWS, 128)
        vc[:, term * 128 : (term + 1) * 128] = vb[term, k].reshape(ROWS, 128)
        for chunk in range(4):
            vt[term, chunk * 128 : (chunk + 1) * 128, :] = vb[term, chunk].reshape(ROWS, 128).T
    block = rows(256 + zhi * 128, 128)
    both = mm(vt[0, block], vc[...])
    vv[...] = both[:, :128] + both[:, 128:] + mm(vt[1, block], vc[:, :128])
    vv_in = [put(vv.at[rows((y - d) % 4 * 32, 32)], rvv.at[d - 1], at_y(-d)) for d in (2, 1, 3)]

    arrived(e_in)
    for half in range(2):
        cols = eb[:, half * 256 : (half + 1) * 256]
        part = mm(vt[0], cols) + mm(vt[1], cols)
        for j in range(2):
            for chunk in range(4):
                tile = part[chunk * 128 : (chunk + 1) * 128, j * 128 : (j + 1) * 128]
                va[chunk, 2 * half + j] = tile[:64]
                vbp[2 * half + j, chunk] = tile[64:]
    v_half = halves(va.at[(y + 2) % 4], hva)
    vb_in = [put(vbp.at[(x + e) % 4], rvb.at[e - 1], at_x(e)) for e in (2, 1, 3)]


    first = len(started)
    px_in, a_in, b_in = [], [], {}

    forward(1)

    project_panel(2)
    x_half = halves(px.at[2], hx)

    project(2)
    a_half = halves(pa.at[2], ha)

    arrived(vv_in)
    svv[...] = vv[rows(y * 32, 32)] + rvv[0] + rvv[1] + rvv[2]
    vvx_in = [put(svv, rvx.at[e - 1], at_x(e)) for e in (2, 1, 3)]

    project_panel(1)

    forward(3)

    project(1)

    px_in.append(send_panel(1))

    v_half[1].wait_recv()
    va[(y + 3) % 4, :2] += hva[0]
    va_in = [put(va.at[(y + 3) % 4], rva.at[0], at_y(-1))]
    v_half[3].wait_recv()
    va[(y + 1) % 4, 2:] += hva[1]
    va_in.append(put(va.at[(y + 1) % 4], rva.at[1], at_y(1)))

    a_in.append(send_lower(1))

    project_panel(3)

    px_in.append(send_panel(3))

    forward(0)

    project(3)

    a_in.append(send_lower(3))

    arrived(vvx_in)
    uv[...] = svv[...] + rvx[0] + rvx[1] + rvx[2]
    uv_in = put(uv, ruv, z_near)

    project_panel(0)

    arrived(va_in)
    sva[...] = va[y] + rva[0] + rva[1]
    va2_in = [put(sva.at[(x + e) % 4], rvxa.at[e - 1], at_x(e)) for e in (2, 1, 3)]
    arrived(vb_in)
    svb[...] = vbp[x] + rvb[0] + rvb[1] + rvb[2]
    vb2_in = [put(svb.at[(y - d) % 4], rvyb.at[d - 1], at_y(-d)) for d in (2, 1, 3)]

    project(0)

    arrived(px_in)
    sx[...] = px[0] + rx[0] + rx[1]
    xz_in = put(sx.at[rows((1 - zlo) * 128, 128)], rzx, z_near)

    own = rows(y * 32, 32)
    uv_in.wait_recv()
    g[zhi, k, own] = uv[...] + ruv[...]
    gy_in = [put(g.at[zhi, k, own], g.at[zhi, k, own], at_y(d)) for d in (2, 1, 3)]

    for copy in started[:first]:
        copy.wait_send()

    xz_in.wait_recv()
    s2x[...] = sx[rows(zlo * 128, 128)] + rzx[...]
    xx_in = [put(s2x, rx2.at[e - 1], at_x(e)) for e in (2, 1, 3)]

    b2_in = []
    for d in (2, 1, 3):
        arrived(b_in[d])
        sb[d] = pb[d, x] + rb[0, d] + rb[1, d] + rb[2, d]
        b2_in.append(put(sb.at[d], ryb.at[d - 1], at_y(-d)))

    arrived(a_in)
    for j in range(4):
        sa[j] = pa[0, j] + ra[0, j] + ra[1, j]
    a2_in = [put(sa.at[(x + e) % 4], rxa.at[e - 1], at_x(e)) for e in (2, 1, 3)]

    arrived(va2_in)
    uz[:64] = sva[x] + rvxa[0] + rvxa[1] + rvxa[2]
    arrived(vb2_in)
    uz[64:] = svb[y] + rvyb[0] + rvyb[1] + rvyb[2]
    uz_in = put(uz, ruz, z_near)

    arrived(gy_in)
    g_far = put(g.at[zhi, k], g.at[zhi, k], z_far)
    g_sib = put(g.at[zhi, k], g.at[zhi, k], sibling)

    arrived(xx_in)
    xv[q] = s2x[...] + rx2[0] + rx2[1] + rx2[2]
    far_in = put(xv.at[q], xv.at[q], z_far)
    sib_in = put(xv.at[q], xv.at[q], sibling)

    uz_in.wait_recv()
    own = rows(y * 128, 128)
    u[own] = uz[...] + ruz[...]
    uy_in = [put(u.at[own], u.at[own], at_y(d)) for d in (2, 1, 3)]

    g_far.wait_recv()
    g_pass = put(g.at[1 - zhi, k], g.at[1 - zhi, k], sibling)

    arrived(b_in[0])
    arrived(b2_in)
    ab[1] = pb[0, x] + rb[0, 0] + rb[1, 0] + rb[2, 0] + ryb[0] + ryb[1] + ryb[2]

    arrived(a2_in)
    ab[0] = sa[x] + rxa[0] + rxa[1] + rxa[2]
    ab_in = put(ab.at[1 - zlo], rab, z_near)

    far_in.wait_recv()
    pass_in = put(xv.at[far], xv.at[far], sibling)

    arrived(uy_in)
    middle_second = exact(t2_ref[...], u[0:256])
    g_sib.wait_recv()
    g_pass.wait_recv()
    lower, upper = middle_second[:128], middle_second[128:]
    inner_first = u[256:512] - jnp.concatenate(
        [exact(g[i, 0], lower) + exact(g[i, 1], upper) for i in range(2)], axis=0
    )
    middle_first = exact(t1_ref[...], inner_first)

    sib_in.wait_recv()
    pass_in.wait_recv()
    total = jnp.zeros((128, 128), F32)
    for j in range(4):
        middle = middle_second if j < 2 else middle_first
        total += exact(xv[j], middle[(j % 2) * 128 : (j % 2 + 1) * 128])
    ab_in.wait_recv()
    out_ref[...] = ab[zlo] + rab[...] - total

    for copy in started[first:]:
        copy.wait_send()


def per_device(tokens, eigvecs, eigvals, v_first, v_second, t_first, t_second):
    vmem = pl.BlockSpec(memory_space=pltpu.VMEM)
    hbm = pl.BlockSpec(memory_space=pltpu.HBM)
    projected = pl.pallas_call(
        kernel,
        out_shape=jax.ShapeDtypeStruct((128, 128), F32),
        in_specs=[hbm, hbm] + [vmem] * 4,
        out_specs=vmem,
        scratch_shapes=[
            pltpu.VMEM((3, 8, YSEG), BF16),
            pltpu.VMEM((4, 4, 8, ROWS), BF16),
            pltpu.VMEM((4, 2, 4, 2, 2, 8, ROWS), BF16),
            pltpu.VMEM((4, 256, ROWS), BF16),
            pltpu.VMEM((SLAB, 128), F32),
            pltpu.VMEM((SLAB, 128), BF16),
            pltpu.VMEM((ROWS, 512), BF16),
            pltpu.VMEM((2, 4, 4, OWN, 128), BF16),
            pltpu.VMEM((2, 512, ROWS), BF16),
            pltpu.VMEM((ROWS, 256), BF16),
            pltpu.VMEM((ROWS, 256), BF16),
            pltpu.VMEM((4, 4, 128, 128), F32),
            pltpu.VMEM((2, 2, 128, 128), F32),
            pltpu.VMEM((2, 4, 128, 128), F32),
            pltpu.VMEM((4, 128, 128), F32),
            pltpu.VMEM((3, 128, 128), F32),
            pltpu.VMEM((4, 4, 128, 128), F32),
            pltpu.VMEM((3, 4, 128, 128), F32),
            pltpu.VMEM((4, 128, 128), F32),
            pltpu.VMEM((3, 128, 128), F32),
            pltpu.VMEM((2, 128, 128), F32),
            pltpu.VMEM((128, 128), F32),
            pltpu.VMEM((4, 256, 128), F32),
            pltpu.VMEM((2, 128, 128), F32),
            pltpu.VMEM((2, 256, 128), F32),
            pltpu.VMEM((256, 128), F32),
            pltpu.VMEM((128, 128), F32),
            pltpu.VMEM((128, 128), F32),
            pltpu.VMEM((3, 128, 128), F32),
            pltpu.VMEM((4, 128, 128), F32),
            pltpu.VMEM((4, 4, 64, 128), F32),
            pltpu.VMEM((2, 2, 64, 128), F32),
            pltpu.VMEM((2, 4, 64, 128), F32),
            pltpu.VMEM((4, 64, 128), F32),
            pltpu.VMEM((3, 64, 128), F32),
            pltpu.VMEM((4, 4, 64, 128), F32),
            pltpu.VMEM((3, 4, 64, 128), F32),
            pltpu.VMEM((4, 64, 128), F32),
            pltpu.VMEM((3, 64, 128), F32),
            pltpu.VMEM((128, 128), F32),
            pltpu.VMEM((128, 128), F32),
            pltpu.VMEM((512, 128), F32),
            pltpu.VMEM((128, 128), F32),
            pltpu.VMEM((3, 32, 128), F32),
            pltpu.VMEM((32, 128), F32),
            pltpu.VMEM((3, 32, 128), F32),
            pltpu.VMEM((32, 128), F32),
            pltpu.VMEM((32, 128), F32),
            pltpu.VMEM((2, 2, 128, 128), F32),
            pltpu.SemaphoreType.DMA((COPIES,)),
            pltpu.SemaphoreType.DMA((COPIES,)),
            pltpu.SemaphoreType.DMA((16,)),
        ],
        compiler_params=pltpu.CompilerParams(
            collective_id=0, has_side_effects=True, vmem_limit_bytes=56 * 1024 * 1024
        ),
    )(tokens, eigvecs, v_first, v_second, t_first, t_second)
    return projected * lax.rsqrt(eigvals)[None, :]


def solution(mesh):
    in_specs = (
        P(("row", "col"), None),
        P("row", "col"),
        P("col"),
        P(("row", "col"), None),
        P(("row", "col"), None),
        P(),
        P(),
    )
    out_specs = P("row", "col")
    return jax.shard_map(
        per_device, mesh=mesh, in_specs=in_specs, out_specs=out_specs, check_vma=False
    )
```

```python
import functools

import jax
import jax.numpy as jnp
from jax import lax
from jax.experimental import pallas as pl
from jax.experimental.pallas import tpu as pltpu
from jax.sharding import PartitionSpec as P

MESH = pl.DeviceIdType.MESH
BF16 = jnp.bfloat16
F32 = jnp.float32
HIGH = lax.Precision.HIGHEST

ROWS = 1664
OWN = 416
SLAB = 6656
YSEG = 2 * SLAB
HALF = ROWS // 2
COPIES = 128


def mm(a, b):
    return jnp.dot(a, b, preferred_element_type=F32)


def exact(a, b):
    return jnp.dot(a, b, precision=HIGH, preferred_element_type=F32)


def kernel(
    x_ref, e_ref, v1_ref, v2_ref, t1_ref, t2_ref, out_ref,
    xy, xs, xb, x2, ef, es, eb, vb, vt, vq, vc,
    pa, ha, ra, sa, rxa, pb, rb, sb, ryb, ab, rab,
    px, hx, rx, sx, rzx, s2x, rx2, xv,
    va, hva, rva, sva, rvxa, vbp, rvb, svb, rvyb, uz, ruz, u,
    vv, rvv, svv, rvx, uv, ruv, g,
    send, recv, local,
):
    r, c = lax.axis_index("row"), lax.axis_index("col")
    y, zlo = r // 2, r % 2
    x, q = c // 4, c % 4
    zhi, k = q // 2, q % 2

    def at_y(d):
        return (((y + d) % 4) * 2 + zlo, c)

    def at_x(d):
        return (r, ((x + d) % 4) * 4 + q)

    z_far = (r, x * 4 + (1 - zhi) * 2 + k)
    z_near = (y * 2 + 1 - zlo, c)
    z_other = (y * 2 + 1 - zlo, x * 4 + (1 - zhi) * 2 + k)
    sibling = (r, x * 4 + zhi * 2 + 1 - k)

    peers = [at_y(1), at_y(2), at_y(3), at_x(1), at_x(2), at_x(3)]
    peers += [z_far, z_near, z_other, sibling]
    barrier = pltpu.get_barrier_semaphore()
    for peer in peers:
        pl.semaphore_signal(barrier, inc=1, device_id=peer, device_id_type=MESH)

    started = []

    def put(src, dst, device):
        slot = len(started)
        copy = pltpu.make_async_remote_copy(
            src_ref=src, dst_ref=dst, send_sem=send.at[slot], recv_sem=recv.at[slot],
            device_id=device, device_id_type=MESH,
        )
        copy.start()
        started.append(copy)
        return copy

    here = []

    def move(src, dst):
        copy = pltpu.make_async_copy(src, dst, local.at[len(here)])
        copy.start()
        here.append(copy)
        return copy

    def arrived(copies):
        for copy in copies:
            copy.wait_recv()

    def rows(start, size):
        return pl.ds(pl.multiple_of(start, size), size)

    loads = [move(e_ref.at[rows(i * ROWS, ROWS)], ef.at[rows(i * ROWS, ROWS)]) for i in range(4)]

    for chunk in range(4):
        panel = v2_ref if chunk < 2 else v1_ref
        value = panel[:, (chunk % 2) * 128 : (chunk % 2 + 1) * 128]
        high = value.astype(BF16)
        vb[0, chunk, q] = high
        vb[1, chunk, q] = (value - high.astype(F32)).astype(BF16)

    pl.semaphore_wait(barrier, len(peers))

    y_in = {}
    for d in (2, 1, 3):
        to = (y + d) % 4
        src = x_ref.at[:, pl.ds(pl.multiple_of(to * YSEG, 128), YSEG)]
        y_in[d] = put(src, xy.at[d - 1], at_y(d))
    v_far = put(vb.at[:, :, q], vb.at[:, :, q], z_far)
    v_sib = put(vb.at[:, :, q], vb.at[:, :, q], sibling)

    def x_stage(d):
        def piece(zl, to):
            at = zl * SLAB + to * ROWS
            if d == 0:
                return x_ref.at[:, pl.ds(pl.multiple_of(y * YSEG + at, 128), ROWS)]
            return xy.at[d - 1, :, pl.ds(pl.multiple_of(at, 128), ROWS)]

        mine, other = xb.at[d, zlo, x, zhi, k], xs.at[d, x]
        waits = []
        for e in (2, 1, 3):
            to = (x + e) % 4
            waits.append(put(piece(zlo, to), mine, at_x(e)))
            waits.append(put(piece(1 - zlo, to), other, at_x(e)))
        return waits, [move(piece(zlo, x), mine), move(piece(1 - zlo, x), other)]

    own_cols = rows(x * 128, 128)

    def e_stage(half):
        waits = []
        for e in (2, 1, 3):
            src = es.at[rows(((x + e) % 4 * 2 + half) * HALF, HALF)]
            waits.append(put(src, eb.at[half * HALF : (half + 1) * HALF, own_cols], at_x(e)))
        return waits

    def z_stage(d):
        block = xb.at[d, zlo, :, zhi, k]
        return [
            put(block, block, z_far),
            put(xs.at[d], block, z_near),
            put(xs.at[d], block, z_other),
        ]

    x_in, z_in, c_in = {}, {}, {}
    x_in[0] = x_stage(0)

    def cast(i, carry):
        at = rows(i * 208, 208)
        es[at] = ef[at].astype(BF16)
        return carry

    def keep(i, carry):
        eb[rows(i * 208, 208), own_cols] = es[rows(x * ROWS + i * 208, 208)]
        return carry

    for copy in loads:
        copy.wait()
    lax.fori_loop(0, 32, cast, 0)
    e_in = e_stage(0)
    lax.fori_loop(0, 8, keep, 0)
    y_in[2].wait_recv()
    x_in[2] = x_stage(2)
    for d in (1, 3):
        y_in[d].wait_recv()
        x_in[d] = x_stage(d)
        if d == 3:
            e_in += e_stage(1)

    def along_z(d):
        arrived(x_in[d][0])
        for copy in x_in[d][1]:
            copy.wait()
        z_in[d] = z_stage(d)

    for d in (2, 1, 3, 0):
        along_z(d)

    def forward(d):
        arrived(z_in[d])
        block = xb.at[d, :, :, :, k]
        c_in[d] = put(block, block, sibling)

    def halves(value, got):
        half = value.shape[0] // 2
        return {
            1: put(value.at[:half], got.at[0], at_y(-1)),
            3: put(value.at[half:], got.at[1], at_y(1)),
        }

    def project_panel(d):
        c_in[d].wait_recv()

        def pack(i, carry):
            value = xb[d, i // 4, i % 4].astype(F32).reshape(32, ROWS)
            x2[d, rows(i * 32, 32)] = value.astype(BF16)
            return carry

        lax.fori_loop(0, 8, pack, 0)
        both = mm(x2[d], vq[...])
        px[d] = both[:, :128] + both[:, 128:]

    def send_panel(d):
        x_half[d].wait_recv()
        if d == 1:
            px[1, :128] += hx[0]
            return put(px.at[1], rx.at[0], at_y(-1))
        px[3, 128:] += hx[1]
        return put(px.at[3], rx.at[1], at_y(1))

    def project(d):
        part = mm(x2[d], eb[...])
        for j in range(4):
            pa[d, j] = part[:128, j * 128 : (j + 1) * 128]
            pb[d, j] = part[128:, j * 128 : (j + 1) * 128]
        b_in[d] = [put(pb.at[d, (x + e) % 4], rb.at[e - 1, d], at_x(e)) for e in (2, 1, 3)]

    def send_lower(d):
        a_half[d].wait_recv()
        if d == 1:
            pa[1, :2] += ha[0]
            return put(pa.at[1], ra.at[0], at_y(-1))
        pa[3, 2:] += ha[1]
        return put(pa.at[3], ra.at[1], at_y(1))

    v_far.wait_recv()
    far = (1 - zhi) * 2 + k
    v_pass = put(vb.at[:, :, far], vb.at[:, :, far], sibling)
    forward(2)
    v_sib.wait_recv()
    v_pass.wait_recv()

    for term in range(2):
        vq[:, term * 128 : (term + 1) * 128] = vb[term, q].reshape(ROWS, 128)
        vc[:, term * 128 : (term + 1) * 128] = vb[term, k].reshape(ROWS, 128)
        for chunk in range(4):
            vt[term, chunk * 128 : (chunk + 1) * 128, :] = vb[term, chunk].reshape(ROWS, 128).T
    block = rows(256 + zhi * 128, 128)
    both = mm(vt[0, block], vc[...])
    vv[...] = both[:, :128] + both[:, 128:] + mm(vt[1, block], vc[:, :128])
    vv_in = [put(vv.at[rows((y - d) % 4 * 32, 32)], rvv.at[d - 1], at_y(-d)) for d in (2, 1, 3)]

    arrived(e_in)
    for half in range(2):
        cols = eb[:, half * 256 : (half + 1) * 256]
        part = mm(vt[0], cols) + mm(vt[1], cols)
        for j in range(2):
            for chunk in range(4):
                tile = part[chunk * 128 : (chunk + 1) * 128, j * 128 : (j + 1) * 128]
                va[chunk, 2 * half + j] = tile[:64]
                vbp[2 * half + j, chunk] = tile[64:]
    v_half = halves(va.at[(y + 2) % 4], hva)
    vb_in = [put(vbp.at[(x + e) % 4], rvb.at[e - 1], at_x(e)) for e in (2, 1, 3)]


    px_in, a_in, b_in = [], [], {}

    forward(1)

    project_panel(2)
    x_half = halves(px.at[2], hx)

    project(2)
    a_half = halves(pa.at[2], ha)

    arrived(vv_in)
    svv[...] = vv[rows(y * 32, 32)] + rvv[0] + rvv[1] + rvv[2]
    vvx_in = [put(svv, rvx.at[e - 1], at_x(e)) for e in (2, 1, 3)]

    project_panel(1)

    forward(3)

    project(1)

    px_in.append(send_panel(1))

    v_half[1].wait_recv()
    va[(y + 3) % 4, :2] += hva[0]
    va_in = [put(va.at[(y + 3) % 4], rva.at[0], at_y(-1))]
    v_half[3].wait_recv()
    va[(y + 1) % 4, 2:] += hva[1]
    va_in.append(put(va.at[(y + 1) % 4], rva.at[1], at_y(1)))

    a_in.append(send_lower(1))

    project_panel(3)

    px_in.append(send_panel(3))

    forward(0)

    project(3)

    a_in.append(send_lower(3))

    arrived(vvx_in)
    uv[...] = svv[...] + rvx[0] + rvx[1] + rvx[2]
    uv_in = put(uv, ruv, z_near)

    project_panel(0)

    arrived(va_in)
    sva[...] = va[y] + rva[0] + rva[1]
    va2_in = [put(sva.at[(x + e) % 4], rvxa.at[e - 1], at_x(e)) for e in (2, 1, 3)]
    arrived(vb_in)
    svb[...] = vbp[x] + rvb[0] + rvb[1] + rvb[2]
    vb2_in = [put(svb.at[(y - d) % 4], rvyb.at[d - 1], at_y(-d)) for d in (2, 1, 3)]

    project(0)

    arrived(px_in)
    sx[...] = px[0] + rx[0] + rx[1]
    xz_in = put(sx.at[rows((1 - zlo) * 128, 128)], rzx, z_near)

    own = rows(y * 32, 32)
    uv_in.wait_recv()
    g[zhi, k, own] = uv[...] + ruv[...]
    gy_in = [put(g.at[zhi, k, own], g.at[zhi, k, own], at_y(d)) for d in (2, 1, 3)]

    b2_in = []
    for d in (2, 1, 3):
        arrived(b_in[d])
        sb[d] = pb[d, x] + rb[0, d] + rb[1, d] + rb[2, d]
        b2_in.append(put(sb.at[d], ryb.at[d - 1], at_y(-d)))

    xz_in.wait_recv()
    s2x[...] = sx[rows(zlo * 128, 128)] + rzx[...]
    xx_in = [put(s2x, rx2.at[e - 1], at_x(e)) for e in (2, 1, 3)]

    arrived(a_in)
    for j in range(4):
        sa[j] = pa[0, j] + ra[0, j] + ra[1, j]
    a2_in = [put(sa.at[(x + e) % 4], rxa.at[e - 1], at_x(e)) for e in (2, 1, 3)]

    arrived(va2_in)
    uz[:64] = sva[x] + rvxa[0] + rvxa[1] + rvxa[2]
    arrived(vb2_in)
    uz[64:] = svb[y] + rvyb[0] + rvyb[1] + rvyb[2]
    uz_in = put(uz, ruz, z_near)

    arrived(gy_in)
    g_far = put(g.at[zhi, k], g.at[zhi, k], z_far)
    g_sib = put(g.at[zhi, k], g.at[zhi, k], sibling)

    arrived(xx_in)
    xv[q] = s2x[...] + rx2[0] + rx2[1] + rx2[2]
    far_in = put(xv.at[q], xv.at[q], z_far)
    sib_in = put(xv.at[q], xv.at[q], sibling)

    uz_in.wait_recv()
    own = rows(y * 128, 128)
    u[own] = uz[...] + ruz[...]
    uy_in = [put(u.at[own], u.at[own], at_y(d)) for d in (2, 1, 3)]

    g_far.wait_recv()
    g_pass = put(g.at[1 - zhi, k], g.at[1 - zhi, k], sibling)

    arrived(b_in[0])
    arrived(b2_in)
    ab[1] = pb[0, x] + rb[0, 0] + rb[1, 0] + rb[2, 0] + ryb[0] + ryb[1] + ryb[2]

    arrived(a2_in)
    ab[0] = sa[x] + rxa[0] + rxa[1] + rxa[2]
    ab_in = put(ab.at[1 - zlo], rab, z_near)

    far_in.wait_recv()
    pass_in = put(xv.at[far], xv.at[far], sibling)

    arrived(uy_in)
    middle_second = exact(t2_ref[...], u[0:256])
    g_sib.wait_recv()
    g_pass.wait_recv()
    lower, upper = middle_second[:128], middle_second[128:]
    inner_first = u[256:512] - jnp.concatenate(
        [exact(g[i, 0], lower) + exact(g[i, 1], upper) for i in range(2)], axis=0
    )
    middle_first = exact(t1_ref[...], inner_first)

    sib_in.wait_recv()
    pass_in.wait_recv()
    total = jnp.zeros((128, 128), F32)
    for j in range(4):
        middle = middle_second if j < 2 else middle_first
        total += exact(xv[j], middle[(j % 2) * 128 : (j % 2 + 1) * 128])
    ab_in.wait_recv()
    out_ref[...] = ab[zlo] + rab[...] - total

    for copy in started:
        copy.wait_send()


def per_device(tokens, eigvecs, eigvals, v_first, v_second, t_first, t_second):
    vmem = pl.BlockSpec(memory_space=pltpu.VMEM)
    hbm = pl.BlockSpec(memory_space=pltpu.HBM)
    projected = pl.pallas_call(
        kernel,
        out_shape=jax.ShapeDtypeStruct((128, 128), F32),
        in_specs=[hbm, hbm] + [vmem] * 4,
        out_specs=vmem,
        scratch_shapes=[
            pltpu.VMEM((3, 8, YSEG), BF16),
            pltpu.VMEM((4, 4, 8, ROWS), BF16),
            pltpu.VMEM((4, 2, 4, 2, 2, 8, ROWS), BF16),
            pltpu.VMEM((4, 256, ROWS), BF16),
            pltpu.VMEM((SLAB, 128), F32),
            pltpu.VMEM((SLAB, 128), BF16),
            pltpu.VMEM((ROWS, 512), BF16),
            pltpu.VMEM((2, 4, 4, OWN, 128), BF16),
            pltpu.VMEM((2, 512, ROWS), BF16),
            pltpu.VMEM((ROWS, 256), BF16),
            pltpu.VMEM((ROWS, 256), BF16),
            pltpu.VMEM((4, 4, 128, 128), F32),
            pltpu.VMEM((2, 2, 128, 128), F32),
            pltpu.VMEM((2, 4, 128, 128), F32),
            pltpu.VMEM((4, 128, 128), F32),
            pltpu.VMEM((3, 128, 128), F32),
            pltpu.VMEM((4, 4, 128, 128), F32),
            pltpu.VMEM((3, 4, 128, 128), F32),
            pltpu.VMEM((4, 128, 128), F32),
            pltpu.VMEM((3, 128, 128), F32),
            pltpu.VMEM((2, 128, 128), F32),
            pltpu.VMEM((128, 128), F32),
            pltpu.VMEM((4, 256, 128), F32),
            pltpu.VMEM((2, 128, 128), F32),
            pltpu.VMEM((2, 256, 128), F32),
            pltpu.VMEM((256, 128), F32),
            pltpu.VMEM((128, 128), F32),
            pltpu.VMEM((128, 128), F32),
            pltpu.VMEM((3, 128, 128), F32),
            pltpu.VMEM((4, 128, 128), F32),
            pltpu.VMEM((4, 4, 64, 128), F32),
            pltpu.VMEM((2, 2, 64, 128), F32),
            pltpu.VMEM((2, 4, 64, 128), F32),
            pltpu.VMEM((4, 64, 128), F32),
            pltpu.VMEM((3, 64, 128), F32),
            pltpu.VMEM((4, 4, 64, 128), F32),
            pltpu.VMEM((3, 4, 64, 128), F32),
            pltpu.VMEM((4, 64, 128), F32),
            pltpu.VMEM((3, 64, 128), F32),
            pltpu.VMEM((128, 128), F32),
            pltpu.VMEM((128, 128), F32),
            pltpu.VMEM((512, 128), F32),
            pltpu.VMEM((128, 128), F32),
            pltpu.VMEM((3, 32, 128), F32),
            pltpu.VMEM((32, 128), F32),
            pltpu.VMEM((3, 32, 128), F32),
            pltpu.VMEM((32, 128), F32),
            pltpu.VMEM((32, 128), F32),
            pltpu.VMEM((2, 2, 128, 128), F32),
            pltpu.SemaphoreType.DMA((COPIES,)),
            pltpu.SemaphoreType.DMA((COPIES,)),
            pltpu.SemaphoreType.DMA((16,)),
        ],
        compiler_params=pltpu.CompilerParams(
            collective_id=0, has_side_effects=True, vmem_limit_bytes=56 * 1024 * 1024
        ),
    )(tokens, eigvecs, v_first, v_second, t_first, t_second)
    return projected * lax.rsqrt(eigvals)[None, :]


def solution(mesh):
    in_specs = (
        P(("row", "col"), None),
        P("row", "col"),
        P("col"),
        P(("row", "col"), None),
        P(("row", "col"), None),
        P(),
        P(),
    )
    out_specs = P("row", "col")
    return jax.shard_map(
        per_device, mesh=mesh, in_specs=in_specs, out_specs=out_specs, check_vma=False
    )
```
